256 devices in a mesh: gx: 16 (over z, y_lo), gz: 8 (over y_hi, x), ta: 2 (over core).
Axes of the slice: x: 4, y: 4 (y_hi: 2, y_lo: 2; y = y_hi * 2 + y_lo), z: 8, core: 2. Of those that a mesh axis runs over, the one named last changes fastest.
Arguments:
- fine_field: bfloat16 [2, 2, 6, 4, 262144], P(None, None, None, None, ('gx', 'gz', 'ta')), may hold values from -6 to 6
- null_vectors: bfloat16 [2, 2, 6, 32, 262144], P(None, None, None, None, ('gx', 'gz', 'ta')), may hold values from -0.21875 to 0.21875
- aggregate: int32 [262144], P(('gx', 'gz', 'ta')), may hold values from 0 to 255
- coarse_links: bfloat16 [32, 2, 16, 4, 9, 64, 128], P('gx', None, 'gz', 'ta'), may hold values from -0.1875 to 0.1875
Outputs:
- prolonged: bfloat16 [2, 2, 6, 4, 262144], P(None, None, None, None, ('gx', 'gz', 'ta'))
The draws below stay inside these ranges and needn't reach their ends.
All inputs are finite; a program needn't handle non-finite values.
Results may differ from the reference program's by a relative error of at most 0.0064.
Values may be sent and summed in bfloat16 or wider, within the bound.
A program may use at most 128 MiB of HBM per device.

```python
import math
import jax
import jax.numpy as jnp
import numpy as np
from jax import lax

NV = 32
NC = 64
SC = 6
RHS = 4
LX = 2
LY = 2
LZ = 2
LT = 2
FS = 1024
CS = 16
NXC = 32
NZC = 16
NTC = 4
FINE = 262144
N_GX = 16
N_GZ = 8
N_TA = 2


def plant(entries, key, smallest, top_value):
    longest = entries.shape.index(max(entries.shape))
    spots = []
    for shift in (0, 1):
        where = [jax.random.randint(jax.random.fold_in(key, axis), (), 0, length) for axis, length in enumerate(entries.shape)]
        where[longest] = (where[longest] + shift) % entries.shape[longest]
        spots.append(tuple(where))
    return entries.at[spots[0]].set(smallest).at[spots[1]].set(top_value)


def block_levels(rng, extent, cuts, smallest, largest):
    def one(dim, blocks):
        heights = jax.random.uniform(jax.random.fold_in(jax.random.fold_in(rng, 6), dim), (blocks,), jnp.float32, smallest / len(cuts), largest / len(cuts))
        return jnp.repeat(jnp.exp(heights), extent[dim] // blocks).reshape((-1,) + (1,) * (len(extent) - dim - 1))

    factor_of = one(*cuts[0])
    for cut in cuts[1:]:
        factor_of = factor_of * one(*cut)
    return factor_of


def cumulative_ranks(number_of, lean):
    loads = [(1 << 20) // math.isqrt(standing ** lean) + 1 for standing in range(1, number_of + 1)]
    spread = 1 + sum(loads) // (1 << 30)
    return np.cumsum(np.array([max(1, weight // spread) for weight in loads]))


def ranked(stream_key, shape, amount, lean):
    table = cumulative_ranks(amount, lean)
    lot = jax.random.randint(jax.random.fold_in(stream_key, 1), shape, 0, int(table[amount - 1]))
    standing = jnp.searchsorted(jnp.asarray(table, jnp.int32), lot, side="right")
    return jax.random.permutation(jax.random.fold_in(stream_key, 2), amount)[standing].astype(jnp.int32)


def scatter_about(key, extent, deviation, bound, split=(), kind=jnp.bfloat16):
    drawn = jax.random.normal(key, extent, jnp.float32) * deviation
    if len(split) > 0:
        drawn = block_levels(key, extent, split, -0.22, 0.18) * drawn
    return jnp.clip(drawn, min=-bound, max=bound).astype(kind)


def setup_inputs(seed: int = 0) -> dict:
    key_list = jax.random.split(jax.random.key(seed), 5)
    fine_field = scatter_about(key_list[0], (2, 2, SC, RHS, FINE), 1.0, 6.0, ((4, 256),))
    null_vectors = scatter_about(key_list[1], (2, 2, SC, NV, FINE), (12 * FS // CS) ** -0.5, 0.21875, ((4, 256),))
    aggregate = plant(ranked(key_list[2], (FINE,), N_GX * CS, 1), jax.random.fold_in(key_list[2], 3), 0, (N_GX * CS) - 1).astype(jnp.int32)
    coarse_links = scatter_about(key_list[3], (NXC, LY, NZC, NTC, 9, NC, 2 * NC), (18 * NC) ** -0.5, 0.1875, ((0, 16), (2, 8), (3, 2)))
    return {"fine_field": fine_field, "null_vectors": null_vectors, "aggregate": aggregate, "coarse_links": coarse_links}


def project_rows(vectors, field):
    real_part = jnp.einsum('cakn,carn->ckrn', vectors[0], field[0]) + jnp.einsum('cakn,carn->ckrn', vectors[1], field[1])
    imag_part = jnp.einsum('cakn,carn->ckrn', vectors[0], field[1]) - jnp.einsum('cakn,carn->ckrn', vectors[1], field[0])
    stacked = jnp.stack([real_part, imag_part])
    return stacked.reshape(-1, stacked.shape[-1]).T


def stack_operand(vectors):
    parts = vectors.reshape(vectors.shape[:-1] + (2, vectors.shape[-1] // (2 * RHS), RHS))
    real_part = parts[..., 0, :, :]
    imag_part = parts[..., 1, :, :]
    real_cols = jnp.concatenate([real_part, -imag_part], axis=-2)
    imag_cols = jnp.concatenate([imag_part, real_part], axis=-2)
    return jnp.concatenate([real_cols, imag_cols], axis=-1)


def finish_vector(summed):
    shaped = summed.reshape(summed.shape[:-1] + (2, RHS))
    shaped = jnp.moveaxis(shaped, -2, -3)
    return shaped.reshape(shaped.shape[:-3] + (-1,))


def global_coarse_index(block_index, agg):
    zindex = (block_index // N_TA) % N_GZ
    tindex = block_index % N_TA
    owner = agg // CS
    local = agg % CS
    pos_x = owner * LX + local // (LY * LZ * LT)
    pos_y = (local // (LZ * LT)) % LY
    pos_z = zindex * LZ + (local // LT) % LZ
    pos_t = tindex * LT + local % LT
    return (((pos_x * LY + pos_y) * NZC + pos_z) * NTC + pos_t).astype(jnp.int32)


def apply_operator(links, vectors):
    neighbours = jnp.stack([
        vectors,
        jnp.roll(vectors, -1, axis=1), jnp.roll(vectors, 1, axis=1),
        jnp.roll(vectors, -1, axis=0), jnp.roll(vectors, 1, axis=0),
        jnp.roll(vectors, -1, axis=2), jnp.roll(vectors, 1, axis=2),
        jnp.roll(vectors, -1, axis=3), jnp.roll(vectors, 1, axis=3)], axis=4)

    def one_slab(pair):
        link_slab, near = pair
        operand = stack_operand(near).astype(jnp.float32)
        summed = jnp.einsum('yztmrk,yztmkj->yztrj', link_slab.astype(jnp.float32), operand)
        return finish_vector(summed)

    return lax.map(one_slab, (links, neighbours))


def reference(fine_field, null_vectors, aggregate, coarse_links):
    ncoarse = NXC * LY * NZC * NTC
    nblocks = fine_field.shape[-1] // FS
    width = 2 * NC * RHS

    def add_block(block_index, accum):
        start = (block_index * FS).astype(jnp.int32)
        vec_block = lax.dynamic_slice_in_dim(null_vectors, start, FS, 4).astype(jnp.float32)
        field_block = lax.dynamic_slice_in_dim(fine_field, start, FS, 4).astype(jnp.float32)
        agg_block = lax.dynamic_slice_in_dim(aggregate, start, FS, 0)
        rows = project_rows(vec_block, field_block)
        target = global_coarse_index(block_index, agg_block)
        return accum + jax.ops.segment_sum(rows, target, num_segments=ncoarse)

    restricted = lax.fori_loop(jnp.int32(0), jnp.int32(nblocks), add_block, jnp.zeros((ncoarse, width), jnp.float32))
    coarse = restricted.astype(jnp.bfloat16).reshape(NXC, LY, NZC, NTC, width)
    first = apply_operator(coarse_links, coarse).astype(jnp.bfloat16)
    second = apply_operator(coarse_links, first).astype(jnp.bfloat16).reshape(ncoarse, width)

    def prolong_block(block_index):
        start = (block_index * FS).astype(jnp.int32)
        vec_block = lax.dynamic_slice_in_dim(null_vectors, start, FS, 4).astype(jnp.float32)
        agg_block = lax.dynamic_slice_in_dim(aggregate, start, FS, 0)
        target = global_coarse_index(block_index, agg_block)
        picked = jnp.take(second, target, axis=0).T.reshape(2, 2, NV, RHS, FS).astype(jnp.float32)
        real_part = jnp.einsum('cakn,ckrn->carn', vec_block[0], picked[0]) - jnp.einsum('cakn,ckrn->carn', vec_block[1], picked[1])
        imag_part = jnp.einsum('cakn,ckrn->carn', vec_block[0], picked[1]) + jnp.einsum('cakn,ckrn->carn', vec_block[1], picked[0])
        return jnp.stack([real_part, imag_part]).astype(jnp.bfloat16)

    blocks_out = lax.map(prolong_block, jnp.arange(nblocks, dtype=jnp.int32))
    moved = jnp.moveaxis(blocks_out, 0, 4)
    return moved.reshape(2, 2, SC, RHS, nblocks * FS)
```

```python
import functools

import jax
import jax.numpy as jnp
from jax import lax
from jax.experimental import pallas as pl
from jax.experimental.pallas import tpu as pltpu
from jax.sharding import PartitionSpec as P

RHS = 4
NV = 32
SC = 6
SITES = 16
LANES = 128
CHUNKS = 2
PER = RHS // CHUNKS
F32 = jnp.float32
BF16 = jnp.bfloat16
NT = (((1,), (1,)), ((), ()))
TN = (((0,), (0,)), ((), ()))


def ring_order(count):
    long = count // 2
    pairs = [(dz, dy) for dz in range(long) for dy in range(2) if (dz, dy) != (0, 0)]
    return sorted(pairs, key=lambda p: -(2 * min(p[0], long - p[0]) + p[1]))


def site_bits(s):
    return (s >> 3) & 1, (s >> 2) & 1, (s >> 1) & 1, s & 1


def site_of(x, y, z, t):
    return ((x * 2 + y) * 2 + z) * 2 + t


def local_terms(s):
    x, y, z, t = site_bits(s)
    return (
        (0, s),
        (1, site_of(x, 1 - y, z, t)),
        (2, site_of(x, 1 - y, z, t)),
        (3 if x == 0 else 4, site_of(1 - x, y, z, t)),
        (5 if z == 0 else 6, site_of(x, y, 1 - z, t)),
        (7 if t == 0 else 8, site_of(x, y, z, 1 - t)),
    )


def remote_terms(s):
    x, y, z, t = site_bits(s)
    return (
        (3, 0, site_of(0, y, z, t)) if x == 1 else (4, 1, site_of(1, y, z, t)),
        (5, 2, site_of(x, y, 0, t)) if z == 1 else (6, 3, site_of(x, y, 1, t)),
        (7, 4, site_of(x, y, z, 0)) if t == 1 else (8, 4, site_of(x, y, z, 1)),
    )


def kernel(
    nx,
    nz,
    agg_hbm,
    field_hbm,
    vec_hbm,
    links_hbm,
    out_hbm,
    agg,
    field,
    field32,
    vec,
    links,
    hot,
    rows,
    part32,
    part,
    got,
    spread,
    faces,
    blocks,
    packed,
    whole,
    picked,
    out32,
    out,
    in_sem,
    out_sem,
    rs_send,
    rs_recv,
    face_send,
    face_recv,
    ag_send,
    ag_recv,
):
    fine = agg.shape[1]
    tiles = fine // LANES
    me = lax.axis_index("gx")
    my_z = lax.axis_index("gz")
    my_t = lax.axis_index("ta")
    order = ring_order(nx)
    long = nx // 2

    loads = [
        pltpu.make_async_copy(agg_hbm, agg, in_sem.at[0]),
        pltpu.make_async_copy(field_hbm, field, in_sem.at[1]),
        pltpu.make_async_copy(vec_hbm.at[:, 0], vec.at[:, 0], in_sem.at[2]),
        pltpu.make_async_copy(vec_hbm.at[:, 1], vec.at[:, 1], in_sem.at[3]),
        pltpu.make_async_copy(links_hbm, links, in_sem.at[4]),
    ]
    for load in loads:
        load.start()

    def member(dz, dy):
        z = lax.rem(lax.div(me, 2) + dz, long)
        y = lax.rem(lax.rem(me, 2) + dy, 2)
        return z * 2 + y

    barrier = pltpu.get_barrier_semaphore()
    neighbours = [
        {"gx": lax.rem(me + 1, nx)},
        {"gx": lax.rem(me + nx - 1, nx)},
        {"gz": lax.rem(my_z + 1, nz)},
        {"gz": lax.rem(my_z + nz - 1, nz)},
        {"ta": 1 - my_t},
    ]
    greeted = [{"gx": member(dz, dy)} for dz, dy in order] + neighbours[2:]
    for device in greeted:
        pl.semaphore_signal(barrier, inc=1, device_id=device, device_id_type=pl.DeviceIdType.MESH)

    loads[0].wait()
    groups = hot.shape[0]

    def hot_tile(i, carry):
        lanes = pl.ds(pl.multiple_of(i * LANES, LANES), LANES)
        site = lax.broadcasted_iota(jnp.int32, (groups, LANES), 0)
        hot[:, lanes] = jnp.where(site == agg[:, lanes], 1.0, 0.0).astype(BF16)
        return carry

    lax.fori_loop(0, tiles, hot_tile, 0)

    loads[1].wait()
    for ri in range(2):
        for chi in range(2):
            for a in range(SC):
                plane = (ri * 2 + chi) * SC + a
                field32[plane, :, :] = field[ri, chi, a].astype(F32)
    loads[2].wait()
    loads[3].wait()

    sends = []
    for c in range(CHUNKS):

        def project(step, carry, c=c):
            chi = lax.div(step, tiles)
            lanes = pl.ds(pl.multiple_of(lax.rem(step, tiles) * LANES, LANES), LANES)
            real = [jnp.zeros((NV, LANES), F32) for _ in range(PER)]
            imag = [jnp.zeros((NV, LANES), F32) for _ in range(PER)]
            for a in range(SC):
                vr = vec[0, chi, a, :, lanes].astype(F32)
                vi = vec[1, chi, a, :, lanes].astype(F32)
                for j in range(PER):
                    r = c * PER + j
                    fr = field32[chi * SC + a, r : r + 1, lanes]
                    fi = field32[(2 + chi) * SC + a, r : r + 1, lanes]
                    real[j] = real[j] + (vr * fr + vi * fi)
                    imag[j] = imag[j] + (vr * fi - vi * fr)
            for j in range(PER):
                base = pl.multiple_of(chi * NV, NV)
                rows[pl.ds(j * LANES + base, NV), lanes] = real[j].astype(BF16)
                rows[pl.ds(j * LANES + 2 * NV + base, NV), lanes] = imag[j].astype(BF16)
            return carry

        lax.fori_loop(0, 2 * tiles, project, 0)
        sums = lax.dot_general(hot[...], rows[...], NT, preferred_element_type=F32)
        part32[c] = sums
        part[c] = sums.astype(BF16)
        if c == 0:
            pl.semaphore_wait(barrier, len(greeted))
        for i, (dz, dy) in enumerate(order):
            peer = member(dz, dy)
            copy = pltpu.make_async_remote_copy(
                src_ref=part.at[c, pl.ds(pl.multiple_of(peer * SITES, SITES), SITES)],
                dst_ref=got.at[c, i],
                send_sem=rs_send.at[c, i],
                recv_sem=rs_recv.at[c, i],
                device_id={"gx": peer},
                device_id_type=pl.DeviceIdType.MESH,
            )
            copy.start()
            sends.append(copy)

    lane = lax.broadcasted_iota(jnp.int32, (8, LANES), 1)
    low = lane < LANES // 2
    low16 = lax.broadcasted_iota(jnp.int32, (SITES, LANES), 1) < LANES // 2
    upper = lax.broadcasted_iota(jnp.int32, (8, LANES), 0) < RHS
    half = LANES // 2

    def expand(values, slot):
        for r in range(RHS):
            v = values[r]
            spread[slot, r * SITES : (r + 1) * SITES, :] = jnp.where(low16, v, -v)
            spread[slot, (RHS + r) * SITES : (RHS + r + 1) * SITES, :] = pltpu.roll(v, half, 1)

    def site_rows(slot, s):
        return spread[slot, pl.ds(s, 2 * RHS, stride=SITES), :]

    def send_faces(k):
        copies = []
        for i, back in enumerate((1, 0, 3, 2, 4)):
            copy = pltpu.make_async_remote_copy(
                src_ref=blocks.at[k],
                dst_ref=faces.at[k, back],
                send_sem=face_send.at[k, i],
                recv_sem=face_recv.at[k, back],
                device_id=neighbours[i],
                device_id_type=pl.DeviceIdType.MESH,
            )
            copy.start()
            copies.append(copy)
        return copies

    def term_product(group, terms):
        total = None
        count = len(terms[0])
        for first in range(0, count, 2):
            pick = range(first, min(first + 2, count))
            left = [jnp.concatenate([terms[j][m][1] for j in range(4)], axis=0).astype(BF16) for m in pick]
            right = []
            for m in pick:
                part_links = []
                for j in range(4):
                    x, y, z, t = site_bits(group * 4 + j)
                    part_links.append(links[x, y, z, t, terms[j][m][0]])
                right.append(jnp.concatenate(part_links, axis=0))
            lhs = left[0] if len(left) == 1 else jnp.concatenate(left, axis=1)
            rhs = right[0] if len(right) == 1 else jnp.concatenate(right, axis=1)
            product = lax.dot_general(lhs, rhs, NT, preferred_element_type=F32)
            total = product if total is None else total + product
        return total

    def apply_operator(k, sites):
        copies = send_faces(k)
        totals = []
        for group in range(4):
            terms = [[(m, sites[n]) for m, n in local_terms(group * 4 + j)] for j in range(4)]
            totals.append(term_product(group, terms))
        for slot in range(5):
            copies[(1, 0, 3, 2, 4)[slot]].wait_recv()
            expand([faces[k, slot, r].astype(F32) for r in range(RHS)], slot)
        result = []
        for group in range(4):
            terms = [
                [(m, site_rows(slot, n)) for m, slot, n in remote_terms(group * 4 + j)] for j in range(4)
            ]
            total = totals[group] + term_product(group, terms)
            for j in range(4):
                block = total[8 * j : 8 * j + 8, LANES * (j // 2) : LANES * (j // 2) + LANES]
                swapped = pltpu.roll(block, RHS, 0)
                signed = jnp.where(upper, -swapped, swapped)
                if j % 2 == 0:
                    new = jnp.where(low, block, pltpu.roll(signed, half, 1))
                else:
                    new = jnp.where(low, pltpu.roll(block, half, 1), signed)
                new = new.astype(BF16).astype(F32)
                s = group * 4 + j
                kept = jnp.where(low, new, -new)
                packed[pl.ds(s, RHS, stride=SITES), :] = kept[:RHS]
                result.append(new)
        for r in range(RHS):
            blocks[k + 1, r] = packed[r * SITES : (r + 1) * SITES, :].astype(BF16)
        return result, copies

    mine = pl.ds(pl.multiple_of(me * SITES, SITES), SITES)
    values = []
    loads[4].wait()
    for c in range(CHUNKS):
        total = part32[c, mine, :]
        for i in range(len(order)):
            sends[c * len(order) + i].wait_recv()
            total = total + got[c, i].astype(F32)
        for j in range(PER):
            rounded = total[:, j * LANES : (j + 1) * LANES].astype(BF16)
            blocks[0, c * PER + j] = rounded
            values.append(rounded.astype(F32))
    expand(values, 5)
    sites = [site_rows(5, s) for s in range(SITES)]
    sites, faces_a = apply_operator(0, sites)
    sites, faces_b = apply_operator(1, sites)

    gathers = []
    for c in range(CHUNKS):
        for i, (dz, dy) in enumerate(order):
            copy = pltpu.make_async_remote_copy(
                src_ref=blocks.at[2, pl.ds(c * PER, PER)],
                dst_ref=whole.at[pl.ds(c * PER, PER), mine],
                send_sem=ag_send.at[c, i],
                recv_sem=ag_recv.at[c, i],
                device_id={"gx": member(dz, dy)},
                device_id_type=pl.DeviceIdType.MESH,
            )
            copy.start()
            gathers.append(copy)
    for r in range(RHS):
        whole[r, mine, :] = blocks[2, r]

    for c in range(CHUNKS):
        for i in range(len(order)):
            gathers[c * len(order) + i].wait_recv()
        for j in range(PER):
            picked[j] = lax.dot_general(whole[c * PER + j], hot[...], TN, preferred_element_type=F32)

        def prolong(step, carry, c=c):
            chi = lax.div(step, tiles)
            lanes = pl.ds(pl.multiple_of(lax.rem(step, tiles) * LANES, LANES), LANES)
            base = pl.multiple_of(chi * NV, NV)
            pr = [picked[j, pl.ds(base, NV), lanes] for j in range(PER)]
            pi = [picked[j, pl.ds(2 * NV + base, NV), lanes] for j in range(PER)]
            for a in range(SC):
                vr = vec[0, chi, a, :, lanes].astype(F32)
                vi = vec[1, chi, a, :, lanes].astype(F32)
                for j in range(PER):
                    r = c * PER + j
                    real = jnp.sum(vr * pr[j] - vi * pi[j], axis=0, keepdims=True)
                    imag = jnp.sum(vr * pi[j] + vi * pr[j], axis=0, keepdims=True)
                    out32[chi * SC + a, r : r + 1, lanes] = real
                    out32[(2 + chi) * SC + a, r : r + 1, lanes] = imag
            return carry

        lax.fori_loop(0, 2 * tiles, prolong, 0)

    for ri in range(2):
        for chi in range(2):
            for a in range(SC):
                out[ri, chi, a] = out32[(ri * 2 + chi) * SC + a].astype(BF16)
    store = pltpu.make_async_copy(out, out_hbm, out_sem)
    store.start()
    for copy in sends + faces_a + faces_b + gathers:
        copy.wait_send()
    store.wait()


def per_device(fine_field, null_vectors, aggregate, coarse_links):
    nx = lax.axis_size("gx")
    nz = lax.axis_size("gz")
    fine = fine_field.shape[-1]
    groups = SITES * nx
    peers = nx - 1
    width = PER * LANES
    anywhere = pl.BlockSpec(memory_space=pl.ANY)
    dma = pltpu.SemaphoreType.DMA
    return pl.pallas_call(
        functools.partial(kernel, nx, nz),
        out_shape=jax.ShapeDtypeStruct(fine_field.shape, BF16),
        in_specs=[anywhere] * 4,
        out_specs=anywhere,
        scratch_shapes=[
            pltpu.VMEM((1, fine), jnp.int32),
            pltpu.VMEM(fine_field.shape, BF16),
            pltpu.VMEM((4 * SC, RHS, fine), F32),
            pltpu.VMEM(null_vectors.shape, BF16),
            pltpu.VMEM(coarse_links.shape, BF16),
            pltpu.VMEM((groups, fine), BF16),
            pltpu.VMEM((width, fine), BF16),
            pltpu.VMEM((CHUNKS, groups, width), F32),
            pltpu.VMEM((CHUNKS, groups, width), BF16),
            pltpu.VMEM((CHUNKS, peers, SITES, width), BF16),
            pltpu.VMEM((6, 2 * RHS * SITES, LANES), F32),
            pltpu.VMEM((2, 5, RHS, SITES, LANES), BF16),
            pltpu.VMEM((3, RHS, SITES, LANES), BF16),
            pltpu.VMEM((RHS * SITES, LANES), F32),
            pltpu.VMEM((RHS, groups, LANES), BF16),
            pltpu.VMEM((PER, LANES, fine), F32),
            pltpu.VMEM((4 * SC, RHS, fine), F32),
            pltpu.VMEM(fine_field.shape, BF16),
            dma((5,)),
            dma,
            dma((CHUNKS, peers)),
            dma((CHUNKS, peers)),
            dma((2, 5)),
            dma((2, 5)),
            dma((CHUNKS, peers)),
            dma((CHUNKS, peers)),
        ],
        compiler_params=pltpu.CompilerParams(
            collective_id=0, has_side_effects=True, vmem_limit_bytes=48 * 1024 * 1024
        ),
        name="coarse_cycle",
    )(aggregate.reshape(1, fine), fine_field, null_vectors, coarse_links)


def solution(mesh):
    in_specs = (
        P(None, None, None, None, ("gx", "gz", "ta")),
        P(None, None, None, None, ("gx", "gz", "ta")),
        P(("gx", "gz", "ta")),
        P("gx", None, "gz", "ta", None, None, None),
    )
    out_specs = P(None, None, None, None, ("gx", "gz", "ta"))
    return jax.shard_map(per_device, mesh=mesh, in_specs=in_specs, out_specs=out_specs, check_vma=False)
```

```python
import functools

import jax
import jax.numpy as jnp
from jax import lax
from jax.experimental import pallas as pl
from jax.experimental.pallas import tpu as pltpu
from jax.sharding import PartitionSpec as P

RHS = 4
NV = 32
SC = 6
SITES = 16
LANES = 128
CHUNKS = 2
PER = RHS // CHUNKS
F32 = jnp.float32
BF16 = jnp.bfloat16
NT = (((1,), (1,)), ((), ()))
TN = (((0,), (0,)), ((), ()))


def ring_order(count):
    long = count // 2
    pairs = [(dz, dy) for dz in range(long) for dy in range(2) if (dz, dy) != (0, 0)]
    return sorted(pairs, key=lambda p: -(2 * min(p[0], long - p[0]) + p[1]))


def site_bits(s):
    return (s >> 3) & 1, (s >> 2) & 1, (s >> 1) & 1, s & 1


def site_of(x, y, z, t):
    return ((x * 2 + y) * 2 + z) * 2 + t


def local_terms(s):
    x, y, z, t = site_bits(s)
    return (
        (0, s),
        (1, site_of(x, 1 - y, z, t)),
        (2, site_of(x, 1 - y, z, t)),
        (3 if x == 0 else 4, site_of(1 - x, y, z, t)),
        (5 if z == 0 else 6, site_of(x, y, 1 - z, t)),
        (7 if t == 0 else 8, site_of(x, y, z, 1 - t)),
    )


def remote_terms(s):
    x, y, z, t = site_bits(s)
    return (
        (3, 0, site_of(0, y, z, t)) if x == 1 else (4, 1, site_of(1, y, z, t)),
        (5, 2, site_of(x, y, 0, t)) if z == 1 else (6, 3, site_of(x, y, 1, t)),
        (7, 4, site_of(x, y, z, 0)) if t == 1 else (8, 4, site_of(x, y, z, 1)),
    )


def kernel(
    nx,
    nz,
    agg_hbm,
    field_hbm,
    vec_hbm,
    links_hbm,
    out_hbm,
    agg,
    field,
    field32,
    vec,
    links,
    hot,
    rows,
    part32,
    part,
    got,
    spread,
    faces,
    blocks,
    packed,
    whole,
    picked,
    out32,
    out,
    in_sem,
    out_sem,
    rs_send,
    rs_recv,
    face_send,
    face_recv,
    ag_send,
    ag_recv,
):
    def await_bytes(ref, sem):
        pltpu.make_async_copy(ref, ref, sem).wait()

    fine = agg.shape[1]
    tiles = fine // LANES
    me = lax.axis_index("gx")
    my_z = lax.axis_index("gz")
    my_t = lax.axis_index("ta")
    order = ring_order(nx)
    long = nx // 2

    loads = [
        pltpu.make_async_copy(agg_hbm, agg, in_sem.at[0]),
        pltpu.make_async_copy(field_hbm, field, in_sem.at[1]),
        pltpu.make_async_copy(vec_hbm.at[:, 0], vec.at[:, 0], in_sem.at[2]),
        pltpu.make_async_copy(vec_hbm.at[:, 1], vec.at[:, 1], in_sem.at[3]),
        pltpu.make_async_copy(links_hbm, links, in_sem.at[4]),
    ]
    for load in loads:
        load.start()

    def member(dz, dy):
        z = lax.rem(lax.div(me, 2) + dz, long)
        y = lax.rem(lax.rem(me, 2) + dy, 2)
        return z * 2 + y

    barrier = pltpu.get_barrier_semaphore()
    neighbours = [
        {"gx": lax.rem(me + 1, nx)},
        {"gx": lax.rem(me + nx - 1, nx)},
        {"gz": lax.rem(my_z + 1, nz)},
        {"gz": lax.rem(my_z + nz - 1, nz)},
        {"ta": 1 - my_t},
    ]
    greeted = [{"gx": member(dz, dy)} for dz, dy in order] + neighbours[2:]
    for device in greeted:
        pl.semaphore_signal(barrier, inc=1, device_id=device, device_id_type=pl.DeviceIdType.MESH)

    loads[0].wait()
    groups = hot.shape[0]

    def hot_tile(i, carry):
        lanes = pl.ds(pl.multiple_of(i * LANES, LANES), LANES)
        site = lax.broadcasted_iota(jnp.int32, (groups, LANES), 0)
        hot[:, lanes] = jnp.where(site == agg[:, lanes], 1.0, 0.0).astype(BF16)
        return carry

    lax.fori_loop(0, tiles, hot_tile, 0)

    loads[1].wait()
    for ri in range(2):
        for chi in range(2):
            for a in range(SC):
                plane = (ri * 2 + chi) * SC + a
                field32[plane, :, :] = field[ri, chi, a].astype(F32)
    loads[2].wait()
    loads[3].wait()

    for c in range(CHUNKS):

        def project(step, carry, c=c):
            chi = lax.div(step, tiles)
            lanes = pl.ds(pl.multiple_of(lax.rem(step, tiles) * LANES, LANES), LANES)
            real = [jnp.zeros((NV, LANES), F32) for _ in range(PER)]
            imag = [jnp.zeros((NV, LANES), F32) for _ in range(PER)]
            for a in range(SC):
                vr = vec[0, chi, a, :, lanes].astype(F32)
                vi = vec[1, chi, a, :, lanes].astype(F32)
                for j in range(PER):
                    r = c * PER + j
                    fr = field32[chi * SC + a, r : r + 1, lanes]
                    fi = field32[(2 + chi) * SC + a, r : r + 1, lanes]
                    real[j] = real[j] + (vr * fr + vi * fi)
                    imag[j] = imag[j] + (vr * fi - vi * fr)
            for j in range(PER):
                base = pl.multiple_of(chi * NV, NV)
                rows[pl.ds(j * LANES + base, NV), lanes] = real[j].astype(BF16)
                rows[pl.ds(j * LANES + 2 * NV + base, NV), lanes] = imag[j].astype(BF16)
            return carry

        lax.fori_loop(0, 2 * tiles, project, 0)
        sums = lax.dot_general(hot[...], rows[...], NT, preferred_element_type=F32)
        part32[c] = sums
        part[c] = sums.astype(BF16)
        if c == 0:
            pl.semaphore_wait(barrier, len(greeted))
        for i, (dz, dy) in enumerate(order):
            peer = member(dz, dy)
            copy = pltpu.make_async_remote_copy(
                src_ref=part.at[c, pl.ds(pl.multiple_of(peer * SITES, SITES), SITES)],
                dst_ref=got.at[c, i],
                send_sem=rs_send.at[c],
                recv_sem=rs_recv.at[c],
                device_id={"gx": peer},
                device_id_type=pl.DeviceIdType.MESH,
            )
            copy.start()

    lane = lax.broadcasted_iota(jnp.int32, (8, LANES), 1)
    low = lane < LANES // 2
    low16 = lax.broadcasted_iota(jnp.int32, (SITES, LANES), 1) < LANES // 2
    upper = lax.broadcasted_iota(jnp.int32, (8, LANES), 0) < RHS
    half = LANES // 2

    def expand(values, slot):
        for r in range(RHS):
            v = values[r]
            spread[slot, r * SITES : (r + 1) * SITES, :] = jnp.where(low16, v, -v)
            spread[slot, (RHS + r) * SITES : (RHS + r + 1) * SITES, :] = pltpu.roll(v, half, 1)

    def site_rows(slot, s):
        return spread[slot, pl.ds(s, 2 * RHS, stride=SITES), :]

    def send_faces(k):
        copies = []
        for i, back in enumerate((1, 0, 3, 2, 4)):
            copy = pltpu.make_async_remote_copy(
                src_ref=blocks.at[k],
                dst_ref=faces.at[k, back],
                send_sem=face_send.at[k],
                recv_sem=face_recv.at[k, back],
                device_id=neighbours[i],
                device_id_type=pl.DeviceIdType.MESH,
            )
            copy.start()
            copies.append(copy)
        return copies

    def term_product(group, terms):
        total = None
        count = len(terms[0])
        for first in range(0, count, 2):
            pick = range(first, min(first + 2, count))
            left = [jnp.concatenate([terms[j][m][1] for j in range(4)], axis=0).astype(BF16) for m in pick]
            right = []
            for m in pick:
                part_links = []
                for j in range(4):
                    x, y, z, t = site_bits(group * 4 + j)
                    part_links.append(links[x, y, z, t, terms[j][m][0]])
                right.append(jnp.concatenate(part_links, axis=0))
            lhs = left[0] if len(left) == 1 else jnp.concatenate(left, axis=1)
            rhs = right[0] if len(right) == 1 else jnp.concatenate(right, axis=1)
            product = lax.dot_general(lhs, rhs, NT, preferred_element_type=F32)
            total = product if total is None else total + product
        return total

    def apply_operator(k, sites):
        copies = send_faces(k)
        totals = []
        for group in range(4):
            terms = [[(m, sites[n]) for m, n in local_terms(group * 4 + j)] for j in range(4)]
            totals.append(term_product(group, terms))
        for slot in range(5):
            copies[(1, 0, 3, 2, 4)[slot]].wait_recv()
            expand([faces[k, slot, r].astype(F32) for r in range(RHS)], slot)
        result = []
        for group in range(4):
            terms = [
                [(m, site_rows(slot, n)) for m, slot, n in remote_terms(group * 4 + j)] for j in range(4)
            ]
            total = totals[group] + term_product(group, terms)
            for j in range(4):
                block = total[8 * j : 8 * j + 8, LANES * (j // 2) : LANES * (j // 2) + LANES]
                swapped = pltpu.roll(block, RHS, 0)
                signed = jnp.where(upper, -swapped, swapped)
                if j % 2 == 0:
                    new = jnp.where(low, block, pltpu.roll(signed, half, 1))
                else:
                    new = jnp.where(low, pltpu.roll(block, half, 1), signed)
                new = new.astype(BF16).astype(F32)
                s = group * 4 + j
                kept = jnp.where(low, new, -new)
                packed[pl.ds(s, RHS, stride=SITES), :] = kept[:RHS]
                result.append(new)
        for r in range(RHS):
            blocks[k + 1, r] = packed[r * SITES : (r + 1) * SITES, :].astype(BF16)
        return result

    mine = pl.ds(pl.multiple_of(me * SITES, SITES), SITES)
    values = []
    loads[4].wait()
    for c in range(CHUNKS):
        total = part32[c, mine, :]
        await_bytes(got.at[c], rs_recv.at[c])
        for i in range(len(order)):
            total = total + got[c, i].astype(F32)
        for j in range(PER):
            rounded = total[:, j * LANES : (j + 1) * LANES].astype(BF16)
            blocks[0, c * PER + j] = rounded
            values.append(rounded.astype(F32))
    expand(values, 5)
    sites = [site_rows(5, s) for s in range(SITES)]
    sites = apply_operator(0, sites)
    apply_operator(1, sites)

    for c in range(CHUNKS):
        for i, (dz, dy) in enumerate(order):
            copy = pltpu.make_async_remote_copy(
                src_ref=blocks.at[2, pl.ds(c * PER, PER)],
                dst_ref=whole.at[pl.ds(c * PER, PER), mine],
                send_sem=ag_send.at[c],
                recv_sem=ag_recv.at[c],
                device_id={"gx": member(dz, dy)},
                device_id_type=pl.DeviceIdType.MESH,
            )
            copy.start()
        pltpu.make_async_copy(
            blocks.at[2, pl.ds(c * PER, PER)], whole.at[pl.ds(c * PER, PER), mine], ag_recv.at[c]
        ).start()

    for c in range(CHUNKS):
        await_bytes(whole.at[pl.ds(c * PER, PER)], ag_recv.at[c])
        for j in range(PER):
            picked[j] = lax.dot_general(whole[c * PER + j], hot[...], TN, preferred_element_type=F32)

        def prolong(step, carry, c=c):
            chi = lax.div(step, tiles)
            lanes = pl.ds(pl.multiple_of(lax.rem(step, tiles) * LANES, LANES), LANES)
            base = pl.multiple_of(chi * NV, NV)
            pr = [picked[j, pl.ds(base, NV), lanes] for j in range(PER)]
            pi = [picked[j, pl.ds(2 * NV + base, NV), lanes] for j in range(PER)]
            for a in range(SC):
                vr = vec[0, chi, a, :, lanes].astype(F32)
                vi = vec[1, chi, a, :, lanes].astype(F32)
                for j in range(PER):
                    r = c * PER + j
                    real = jnp.sum(vr * pr[j] - vi * pi[j], axis=0, keepdims=True)
                    imag = jnp.sum(vr * pi[j] + vi * pr[j], axis=0, keepdims=True)
                    out32[chi * SC + a, r : r + 1, lanes] = real
                    out32[(2 + chi) * SC + a, r : r + 1, lanes] = imag
            return carry

        lax.fori_loop(0, 2 * tiles, prolong, 0)

    for ri in range(2):
        for chi in range(2):
            for a in range(SC):
                out[ri, chi, a] = out32[(ri * 2 + chi) * SC + a].astype(BF16)
    store = pltpu.make_async_copy(out, out_hbm, out_sem)
    store.start()
    for c in range(CHUNKS):
        await_bytes(got.at[c], rs_send.at[c])
        await_bytes(whole.at[pl.ds(c * PER, PER), pl.ds(0, groups - SITES)], ag_send.at[c])
    for k in range(2):
        await_bytes(faces.at[k], face_send.at[k])
    store.wait()


def per_device(fine_field, null_vectors, aggregate, coarse_links):
    nx = lax.axis_size("gx")
    nz = lax.axis_size("gz")
    fine = fine_field.shape[-1]
    groups = SITES * nx
    peers = nx - 1
    width = PER * LANES
    anywhere = pl.BlockSpec(memory_space=pl.ANY)
    dma = pltpu.SemaphoreType.DMA
    return pl.pallas_call(
        functools.partial(kernel, nx, nz),
        out_shape=jax.ShapeDtypeStruct(fine_field.shape, BF16),
        in_specs=[pl.BlockSpec(memory_space=pltpu.HBM)] * 4,
        out_specs=anywhere,
        scratch_shapes=[
            pltpu.VMEM((1, fine), jnp.int32),
            pltpu.VMEM(fine_field.shape, BF16),
            pltpu.VMEM((4 * SC, RHS, fine), F32),
            pltpu.VMEM(null_vectors.shape, BF16),
            pltpu.VMEM(coarse_links.shape, BF16),
            pltpu.VMEM((groups, fine), BF16),
            pltpu.VMEM((width, fine), BF16),
            pltpu.VMEM((CHUNKS, groups, width), F32),
            pltpu.VMEM((CHUNKS, groups, width), BF16),
            pltpu.VMEM((CHUNKS, peers, SITES, width), BF16),
            pltpu.VMEM((6, 2 * RHS * SITES, LANES), F32),
            pltpu.VMEM((2, 5, RHS, SITES, LANES), BF16),
            pltpu.VMEM((3, RHS, SITES, LANES), BF16),
            pltpu.VMEM((RHS * SITES, LANES), F32),
            pltpu.VMEM((RHS, groups, LANES), BF16),
            pltpu.VMEM((PER, LANES, fine), F32),
            pltpu.VMEM((4 * SC, RHS, fine), F32),
            pltpu.VMEM(fine_field.shape, BF16),
            dma((5,)),
            dma,
            dma((CHUNKS,)),
            dma((CHUNKS,)),
            dma((2,)),
            dma((2, 5)),
            dma((CHUNKS,)),
            dma((CHUNKS,)),
        ],
        compiler_params=pltpu.CompilerParams(
            collective_id=0, has_side_effects=True
        ),
        name="coarse_cycle",
    )(aggregate.reshape(1, fine), fine_field, null_vectors, coarse_links)


def solution(mesh):
    in_specs = (
        P(None, None, None, None, ("gx", "gz", "ta")),
        P(None, None, None, None, ("gx", "gz", "ta")),
        P(("gx", "gz", "ta")),
        P("gx", None, "gz", "ta", None, None, None),
    )
    out_specs = P(None, None, None, None, ("gx", "gz", "ta"))
    return jax.shard_map(per_device, mesh=mesh, in_specs=in_specs, out_specs=out_specs, check_vma=False)
```

```python
import functools

import jax
import jax.numpy as jnp
from jax import lax
from jax.experimental import pallas as pl
from jax.experimental.pallas import tpu as pltpu
from jax.sharding import PartitionSpec as P

RHS = 4
NV = 32
SC = 6
SITES = 16
LANES = 128
BACK = (1, 0, 3, 2, 4)
FAR_FIRST = (2, 3, 0, 1, 4)
F32 = jnp.float32
BF16 = jnp.bfloat16
NT = (((1,), (1,)), ((), ()))
TN = (((0,), (0,)), ((), ()))


def ring_order(count):
    long = count // 2
    pairs = [(dz, dy) for dz in range(long) for dy in range(2) if (dz, dy) != (0, 0)]
    return sorted(pairs, key=lambda p: -(2 * min(p[0], long - p[0]) + p[1]))


def site_bits(s):
    return (s >> 3) & 1, (s >> 2) & 1, (s >> 1) & 1, s & 1


def site_of(x, y, z, t):
    return ((x * 2 + y) * 2 + z) * 2 + t


def local_terms(s):
    x, y, z, t = site_bits(s)
    return (
        (0, s),
        (1, site_of(x, 1 - y, z, t)),
        (2, site_of(x, 1 - y, z, t)),
        (3 if x == 0 else 4, site_of(1 - x, y, z, t)),
        (5 if z == 0 else 6, site_of(x, y, 1 - z, t)),
        (7 if t == 0 else 8, site_of(x, y, z, 1 - t)),
    )


def remote_terms(s):
    x, y, z, t = site_bits(s)
    return (
        (3, 0, site_of(0, y, z, t)) if x == 1 else (4, 1, site_of(1, y, z, t)),
        (5, 2, site_of(x, y, 0, t)) if z == 1 else (6, 3, site_of(x, y, 1, t)),
        (7, 4, site_of(x, y, z, 0)) if t == 1 else (8, 4, site_of(x, y, z, 1)),
    )


def kernel(
    nx,
    nz,
    agg_hbm,
    field_hbm,
    vec_hbm,
    links_hbm,
    out,
    agg,
    field,
    field32,
    vec,
    links,
    hot,
    rows,
    part,
    got,
    spread,
    faces,
    blocks,
    packed,
    whole,
    picked,
    in_sem,
    rs_send,
    rs_recv,
    face_send,
    face_recv,
    ag_send,
    ag_recv,
):
    def await_bytes(ref, sem):
        pltpu.make_async_copy(ref, ref, sem).wait()

    fine = agg.shape[1]
    tiles = fine // LANES
    me = lax.axis_index("gx")
    my_z = lax.axis_index("gz")
    my_t = lax.axis_index("ta")
    order = ring_order(nx)
    long = nx // 2

    loads = [
        pltpu.make_async_copy(agg_hbm, agg, in_sem.at[0]),
        pltpu.make_async_copy(field_hbm, field, in_sem.at[1]),
        pltpu.make_async_copy(vec_hbm.at[:, 0], vec.at[:, 0], in_sem.at[2]),
        pltpu.make_async_copy(vec_hbm.at[:, 1], vec.at[:, 1], in_sem.at[3]),
        pltpu.make_async_copy(links_hbm, links, in_sem.at[4]),
    ]
    for load in loads[:4]:
        load.start()

    def member(dz, dy):
        z = lax.rem(lax.div(me, 2) + dz, long)
        y = lax.rem(lax.rem(me, 2) + dy, 2)
        return z * 2 + y

    barrier = pltpu.get_barrier_semaphore()
    neighbours = [
        {"gx": lax.rem(me + 1, nx)},
        {"gx": lax.rem(me + nx - 1, nx)},
        {"gz": lax.rem(my_z + 1, nz)},
        {"gz": lax.rem(my_z + nz - 1, nz)},
        {"ta": 1 - my_t},
    ]
    greeted = [{"gx": member(dz, dy)} for dz, dy in order] + neighbours[2:]
    for device in greeted:
        pl.semaphore_signal(barrier, inc=1, device_id=device, device_id_type=pl.DeviceIdType.MESH)

    loads[0].wait()
    groups = hot.shape[0]

    def hot_tile(i, carry):
        lanes = pl.ds(pl.multiple_of(i * LANES, LANES), LANES)
        site = lax.broadcasted_iota(jnp.int32, (groups, LANES), 0)
        hot[:, lanes] = jnp.where(site == agg[:, lanes], 1.0, 0.0).astype(BF16)
        return carry

    lax.fori_loop(0, tiles, hot_tile, 0)

    loads[1].wait()
    for chi in range(2):
        for a in range(SC):
            plane = chi * SC + a
            fr = field[0, chi, a].astype(F32)
            fi = field[1, chi, a].astype(F32)
            field32[plane] = fr
            field32[2 * SC + plane] = fi
            field32[4 * SC + plane] = fr + fi
    loads[2].wait()
    loads[3].wait()

    loads[4].start()

    def project(step, carry):
        chi = lax.div(step, tiles)
        lanes = pl.ds(pl.multiple_of(lax.rem(step, tiles) * LANES, LANES), LANES)
        height = NV // 2
        for part_of in range(2):
            zero = jnp.zeros((height, LANES), F32)
            both, less, more = [zero] * RHS, [zero] * RHS, [zero] * RHS
            for a in range(SC):
                plane = chi * SC + a
                vr = vec[0, chi, a, part_of * height : (part_of + 1) * height, lanes].astype(F32)
                vi = vec[1, chi, a, part_of * height : (part_of + 1) * height, lanes].astype(F32)
                diff, total = vr - vi, vr + vi
                for r in range(RHS):
                    fr = field32[plane, r : r + 1, lanes]
                    fi = field32[2 * SC + plane, r : r + 1, lanes]
                    fs = field32[4 * SC + plane, r : r + 1, lanes]
                    both[r] = both[r] + vr * fs
                    less[r] = less[r] + diff * fi
                    more[r] = more[r] + total * fr
            base = pl.multiple_of(chi * NV + part_of * height, height)
            for r in range(RHS):
                rows[pl.ds(r * LANES + base, height), lanes] = (both[r] - less[r]).astype(BF16)
                rows[pl.ds(r * LANES + 2 * NV + base, height), lanes] = (both[r] - more[r]).astype(BF16)
        return carry

    lax.fori_loop(0, 2 * tiles, project, 0)
    part[...] = lax.dot_general(hot[...], rows[...], NT, preferred_element_type=F32).astype(BF16)
    pl.semaphore_wait(barrier, len(greeted))
    for i, (dz, dy) in enumerate(order):
        peer = member(dz, dy)
        pltpu.make_async_remote_copy(
            src_ref=part.at[pl.ds(pl.multiple_of(peer * SITES, SITES), SITES)],
            dst_ref=got.at[i],
            send_sem=rs_send,
            recv_sem=rs_recv,
            device_id={"gx": peer},
            device_id_type=pl.DeviceIdType.MESH,
        ).start()

    lane = lax.broadcasted_iota(jnp.int32, (8, LANES), 1)
    low = lane < LANES // 2
    low16 = lax.broadcasted_iota(jnp.int32, (SITES, LANES), 1) < LANES // 2
    upper = lax.broadcasted_iota(jnp.int32, (8, LANES), 0) < RHS
    half = LANES // 2

    def expand(values, slot):
        for r in range(RHS):
            v = values[r]
            spread[slot, r * SITES : (r + 1) * SITES, :] = jnp.where(low16, v, -v)
            spread[slot, (RHS + r) * SITES : (RHS + r + 1) * SITES, :] = pltpu.roll(v, half, 1)

    def site_rows(slot, s):
        return spread[slot, pl.ds(s, 2 * RHS, stride=SITES), :]

    def send_faces(k):
        copies = {}
        for i in FAR_FIRST:
            back = BACK[i]
            copy = pltpu.make_async_remote_copy(
                src_ref=blocks.at[k],
                dst_ref=faces.at[k, back],
                send_sem=face_send.at[k],
                recv_sem=face_recv.at[k, back],
                device_id=neighbours[i],
                device_id_type=pl.DeviceIdType.MESH,
            )
            copy.start()
            copies[back] = copy
        return copies

    def term_product(group, terms):
        total = None
        count = len(terms[0])
        for first in range(0, count, 2):
            pick = range(first, min(first + 2, count))
            left = [jnp.concatenate([terms[j][m][1] for j in range(4)], axis=0).astype(BF16) for m in pick]
            right = []
            for m in pick:
                part_links = []
                for j in range(4):
                    x, y, z, t = site_bits(group * 4 + j)
                    part_links.append(links[x, y, z, t, terms[j][m][0]])
                right.append(jnp.concatenate(part_links, axis=0))
            lhs = left[0] if len(left) == 1 else jnp.concatenate(left, axis=1)
            rhs = right[0] if len(right) == 1 else jnp.concatenate(right, axis=1)
            product = lax.dot_general(lhs, rhs, NT, preferred_element_type=F32)
            total = product if total is None else total + product
        return total

    def apply_operator(k, sites):
        copies = send_faces(k)
        totals = []
        for group in range(4):
            terms = [[(m, sites[n]) for m, n in local_terms(group * 4 + j)] for j in range(4)]
            totals.append(term_product(group, terms))
        for slots, which in (((4, 0, 1), (0, 2)), ((2, 3), (1,))):
            for slot in slots:
                copies[slot].wait_recv()
                block = faces[k, slot].astype(F32)
                expand([block[:, r * LANES : (r + 1) * LANES] for r in range(RHS)], slot)
            for group in range(4):
                terms = []
                for j in range(4):
                    remote = remote_terms(group * 4 + j)
                    terms.append([(remote[w][0], site_rows(remote[w][1], remote[w][2])) for w in which])
                totals[group] = totals[group] + term_product(group, terms)
        result = []
        for group in range(4):
            total = totals[group]
            for j in range(4):
                block = total[8 * j : 8 * j + 8, LANES * (j // 2) : LANES * (j // 2) + LANES]
                swapped = pltpu.roll(block, RHS, 0)
                signed = jnp.where(upper, -swapped, swapped)
                if j % 2 == 0:
                    new = jnp.where(low, block, pltpu.roll(signed, half, 1))
                else:
                    new = jnp.where(low, pltpu.roll(block, half, 1), signed)
                new = new.astype(BF16).astype(F32)
                s = group * 4 + j
                kept = jnp.where(low, new, -new)
                packed[pl.ds(s, RHS, stride=SITES), :] = kept[:RHS]
                result.append(new)
        for r in range(RHS):
            blocks[k + 1, :, r * LANES : (r + 1) * LANES] = packed[r * SITES : (r + 1) * SITES, :].astype(BF16)
        return result

    mine = pl.ds(pl.multiple_of(me * SITES, SITES), SITES)
    values = []
    loads[4].wait()
    await_bytes(got, rs_recv)
    for r in range(RHS):
        lanes = slice(r * LANES, (r + 1) * LANES)
        total = part[mine, lanes].astype(F32)
        for i in range(len(order)):
            total = total + got[i, :, lanes].astype(F32)
        rounded = total.astype(BF16)
        blocks[0, :, lanes] = rounded
        values.append(rounded.astype(F32))
    expand(values, 5)
    sites = [site_rows(5, s) for s in range(SITES)]
    sites = apply_operator(0, sites)
    apply_operator(1, sites)

    for dz, dy in order:
        pltpu.make_async_remote_copy(
            src_ref=blocks.at[2],
            dst_ref=whole.at[mine],
            send_sem=ag_send,
            recv_sem=ag_recv,
            device_id={"gx": member(dz, dy)},
            device_id_type=pl.DeviceIdType.MESH,
        ).start()
    pltpu.make_async_copy(blocks.at[2], whole.at[mine], ag_recv).start()

    depth = 2 * NV * RHS
    row = lax.broadcasted_iota(jnp.int32, (2 * RHS, depth), 0)
    column = lax.broadcasted_iota(jnp.int32, (2 * RHS, depth), 1)
    wanted = (column >> 6) + ((column >> 5) & 1) * RHS
    signs = jnp.where(row == wanted, 1.0, 0.0).astype(BF16)

    await_bytes(whole, ag_recv)
    picked[...] = lax.dot_general(whole[...], hot[...], TN, preferred_element_type=F32).astype(BF16)
    wide = 2 * LANES
    steps = fine // wide

    def prolong(step, carry):
        chi = lax.div(step, steps)
        lanes = pl.ds(pl.multiple_of(lax.rem(step, steps) * wide, wide), wide)
        base = pl.multiple_of(chi * NV, NV)
        pr = [picked[pl.ds(r * LANES + base, NV), lanes] for r in range(RHS)]
        pi = [picked[pl.ds(r * LANES + 2 * NV + base, NV), lanes] for r in range(RHS)]
        for a in range(SC):
            vr = vec[0, chi, a, :, lanes]
            vi = vec[1, chi, a, :, lanes]
            products = []
            for r in range(RHS):
                products += [vr * pr[r] - vi * pi[r], vr * pi[r] + vi * pr[r]]
            both = jnp.dot(signs, jnp.concatenate(products, axis=0), preferred_element_type=F32)
            out[0, chi, a, :, lanes] = both[:RHS].astype(BF16)
            out[1, chi, a, :, lanes] = both[RHS:].astype(BF16)
        return carry

    lax.fori_loop(0, 2 * steps, prolong, 0)
    await_bytes(got, rs_send)
    await_bytes(whole.at[pl.ds(0, groups - SITES)], ag_send)
    for k in range(2):
        await_bytes(faces.at[k], face_send.at[k])


def per_device(fine_field, null_vectors, aggregate, coarse_links):
    nx = lax.axis_size("gx")
    nz = lax.axis_size("gz")
    fine = fine_field.shape[-1]
    groups = SITES * nx
    peers = nx - 1
    width = RHS * LANES
    dma = pltpu.SemaphoreType.DMA
    return pl.pallas_call(
        functools.partial(kernel, nx, nz),
        out_shape=jax.ShapeDtypeStruct(fine_field.shape, BF16),
        in_specs=[pl.BlockSpec(memory_space=pltpu.HBM)] * 4,
        out_specs=pl.BlockSpec(memory_space=pltpu.VMEM),
        scratch_shapes=[
            pltpu.VMEM((1, fine), jnp.int32),
            pltpu.VMEM(fine_field.shape, BF16),
            pltpu.VMEM((6 * SC, RHS, fine), F32),
            pltpu.VMEM(null_vectors.shape, BF16),
            pltpu.VMEM(coarse_links.shape, BF16),
            pltpu.VMEM((groups, fine), BF16),
            pltpu.VMEM((width, fine), BF16),
            pltpu.VMEM((groups, width), BF16),
            pltpu.VMEM((peers, SITES, width), BF16),
            pltpu.VMEM((6, 2 * RHS * SITES, LANES), F32),
            pltpu.VMEM((2, 5, SITES, RHS * LANES), BF16),
            pltpu.VMEM((3, SITES, RHS * LANES), BF16),
            pltpu.VMEM((RHS * SITES, LANES), F32),
            pltpu.VMEM((groups, RHS * LANES), BF16),
            pltpu.VMEM((RHS * LANES, fine), BF16),
            dma((5,)),
            dma,
            dma,
            dma((2,)),
            dma((2, 5)),
            dma,
            dma,
        ],
        compiler_params=pltpu.CompilerParams(
            collective_id=0, has_side_effects=True, vmem_limit_bytes=48 * 1024 * 1024
        ),
        name="coarse_cycle",
    )(*[pltpu.with_memory_space_constraint(v, pltpu.HBM) for v in (aggregate.reshape(1, fine), fine_field, null_vectors, coarse_links)])


def solution(mesh):
    in_specs = (
        P(None, None, None, None, ("gx", "gz", "ta")),
        P(None, None, None, None, ("gx", "gz", "ta")),
        P(("gx", "gz", "ta")),
        P("gx", None, "gz", "ta", None, None, None),
    )
    out_specs = P(None, None, None, None, ("gx", "gz", "ta"))
    return jax.shard_map(per_device, mesh=mesh, in_specs=in_specs, out_specs=out_specs, check_vma=False)
```

```python
import functools

import jax
import jax.numpy as jnp
from jax import lax
from jax.experimental import pallas as pl
from jax.experimental.pallas import tpu as pltpu
from jax.sharding import PartitionSpec as P

RHS = 4
NV = 32
SC = 6
SITES = 16
LANES = 128
BACK = (1, 0, 3, 2, 4)
FAR_FIRST = (2, 3, 0, 1, 4)
F32 = jnp.float32
BF16 = jnp.bfloat16
NT = (((1,), (1,)), ((), ()))
TN = (((0,), (0,)), ((), ()))


def ring_order(count):
    long = count // 2
    pairs = [(dz, dy) for dz in range(long) for dy in range(2) if (dz, dy) != (0, 0)]
    return sorted(pairs, key=lambda p: -(2 * min(p[0], long - p[0]) + p[1]))


def site_bits(s):
    return (s >> 3) & 1, (s >> 2) & 1, (s >> 1) & 1, s & 1


def site_of(x, y, z, t):
    return ((x * 2 + y) * 2 + z) * 2 + t


def local_terms(s):
    x, y, z, t = site_bits(s)
    return (
        (0, s),
        (1, site_of(x, 1 - y, z, t)),
        (2, site_of(x, 1 - y, z, t)),
        (3 if x == 0 else 4, site_of(1 - x, y, z, t)),
        (5 if z == 0 else 6, site_of(x, y, 1 - z, t)),
        (7 if t == 0 else 8, site_of(x, y, z, 1 - t)),
    )


def remote_terms(s):
    x, y, z, t = site_bits(s)
    return (
        (3, 0, site_of(0, y, z, t)) if x == 1 else (4, 1, site_of(1, y, z, t)),
        (5, 2, site_of(x, y, 0, t)) if z == 1 else (6, 3, site_of(x, y, 1, t)),
        (7, 4, site_of(x, y, z, 0)) if t == 1 else (8, 4, site_of(x, y, z, 1)),
    )


def kernel(
    nx,
    nz,
    agg_hbm,
    field_hbm,
    vec_hbm,
    links_hbm,
    out,
    agg,
    field,
    field32,
    vec,
    links,
    hot,
    rows,
    part,
    got,
    spread,
    faces,
    blocks,
    packed,
    whole,
    picked,
    in_sem,
    rs_send,
    rs_recv,
    face_send,
    face_recv,
    ag_send,
    ag_recv,
):
    def await_bytes(ref, sem):
        pltpu.make_async_copy(ref, ref, sem).wait()

    fine = agg.shape[1]
    tiles = fine // LANES
    me = lax.axis_index("gx")
    my_z = lax.axis_index("gz")
    my_t = lax.axis_index("ta")
    order = ring_order(nx)
    long = nx // 2

    loads = [
        pltpu.make_async_copy(agg_hbm, agg, in_sem.at[0]),
        pltpu.make_async_copy(field_hbm, field, in_sem.at[1]),
        pltpu.make_async_copy(vec_hbm.at[:, 0], vec.at[:, 0], in_sem.at[2]),
        pltpu.make_async_copy(vec_hbm.at[:, 1], vec.at[:, 1], in_sem.at[3]),
        pltpu.make_async_copy(links_hbm, links, in_sem.at[4]),
    ]
    for load in loads[:4]:
        load.start()

    def member(dz, dy):
        z = lax.rem(lax.div(me, 2) + dz, long)
        y = lax.rem(lax.rem(me, 2) + dy, 2)
        return z * 2 + y

    barrier = pltpu.get_barrier_semaphore()
    neighbours = [
        {"gx": lax.rem(me + 1, nx)},
        {"gx": lax.rem(me + nx - 1, nx)},
        {"gz": lax.rem(my_z + 1, nz)},
        {"gz": lax.rem(my_z + nz - 1, nz)},
        {"ta": 1 - my_t},
    ]
    greeted = [{"gx": member(dz, dy)} for dz, dy in order] + neighbours[2:]
    for device in greeted:
        pl.semaphore_signal(barrier, inc=1, device_id=device, device_id_type=pl.DeviceIdType.MESH)

    loads[0].wait()
    groups = hot.shape[0]

    def hot_tile(i, carry):
        lanes = pl.ds(pl.multiple_of(i * LANES, LANES), LANES)
        site = lax.broadcasted_iota(jnp.int32, (groups, LANES), 0)
        hot[:, lanes] = jnp.where(site == agg[:, lanes], 1.0, 0.0).astype(BF16)
        return carry

    lax.fori_loop(0, tiles, hot_tile, 0)

    loads[1].wait()
    for chi in range(2):
        for a in range(SC):
            plane = chi * SC + a
            fr = field[0, chi, a].astype(F32)
            fi = field[1, chi, a].astype(F32)
            field32[plane] = fr
            field32[2 * SC + plane] = fi
            field32[4 * SC + plane] = fr + fi
    loads[2].wait()
    loads[3].wait()

    loads[4].start()

    def project(step, carry):
        chi = lax.div(step, tiles)
        lanes = pl.ds(pl.multiple_of(lax.rem(step, tiles) * LANES, LANES), LANES)
        height = NV // 2
        for part_of in range(2):
            zero = jnp.zeros((height, LANES), F32)
            both, less, more = [zero] * RHS, [zero] * RHS, [zero] * RHS
            for a in range(SC):
                plane = chi * SC + a
                vr = vec[0, chi, a, part_of * height : (part_of + 1) * height, lanes].astype(F32)
                vi = vec[1, chi, a, part_of * height : (part_of + 1) * height, lanes].astype(F32)
                diff, total = vr - vi, vr + vi
                for r in range(RHS):
                    fr = field32[plane, r : r + 1, lanes]
                    fi = field32[2 * SC + plane, r : r + 1, lanes]
                    fs = field32[4 * SC + plane, r : r + 1, lanes]
                    both[r] = both[r] + vr * fs
                    less[r] = less[r] + diff * fi
                    more[r] = more[r] + total * fr
            base = pl.multiple_of(chi * NV + part_of * height, height)
            for r in range(RHS):
                rows[pl.ds(r * LANES + base, height), lanes] = (both[r] - less[r]).astype(BF16)
                rows[pl.ds(r * LANES + 2 * NV + base, height), lanes] = (both[r] - more[r]).astype(BF16)
        return carry

    lax.fori_loop(0, 2 * tiles, project, 0)
    part[...] = lax.dot_general(hot[...], rows[...], NT, preferred_element_type=F32).astype(BF16)
    pl.semaphore_wait(barrier, len(greeted))
    for i, (dz, dy) in enumerate(order):
        peer = member(dz, dy)
        pltpu.make_async_remote_copy(
            src_ref=part.at[pl.ds(pl.multiple_of(peer * SITES, SITES), SITES)],
            dst_ref=got.at[i],
            send_sem=rs_send,
            recv_sem=rs_recv,
            device_id={"gx": peer},
            device_id_type=pl.DeviceIdType.MESH,
        ).start()

    lane = lax.broadcasted_iota(jnp.int32, (8, LANES), 1)
    low = lane < LANES // 2
    low16 = lax.broadcasted_iota(jnp.int32, (SITES, LANES), 1) < LANES // 2
    upper = lax.broadcasted_iota(jnp.int32, (8, LANES), 0) < RHS
    half = LANES // 2

    def expand(values, slot):
        for r in range(RHS):
            v = values[r]
            spread[slot, r * SITES : (r + 1) * SITES, :] = jnp.where(low16, v, -v)
            spread[slot, (RHS + r) * SITES : (RHS + r + 1) * SITES, :] = pltpu.roll(v, half, 1)

    def site_rows(slot, s):
        return spread[slot, pl.ds(s, 2 * RHS, stride=SITES), :]

    def send_faces(k):
        copies = {}
        for i in FAR_FIRST:
            back = BACK[i]
            copy = pltpu.make_async_remote_copy(
                src_ref=blocks.at[k],
                dst_ref=faces.at[k, back],
                send_sem=face_send.at[k],
                recv_sem=face_recv.at[k, back],
                device_id=neighbours[i],
                device_id_type=pl.DeviceIdType.MESH,
            )
            copy.start()
            copies[back] = copy
        return copies

    def term_product(group, terms):
        total = None
        count = len(terms[0])
        for first in range(0, count, 2):
            pick = range(first, min(first + 2, count))
            left = [jnp.concatenate([terms[j][m][1] for j in range(4)], axis=0).astype(BF16) for m in pick]
            right = []
            for m in pick:
                part_links = []
                for j in range(4):
                    x, y, z, t = site_bits(group * 4 + j)
                    part_links.append(links[x, y, z, t, terms[j][m][0]])
                right.append(jnp.concatenate(part_links, axis=0))
            lhs = left[0] if len(left) == 1 else jnp.concatenate(left, axis=1)
            rhs = right[0] if len(right) == 1 else jnp.concatenate(right, axis=1)
            product = lax.dot_general(lhs, rhs, NT, preferred_element_type=F32)
            total = product if total is None else total + product
        return total

    def apply_operator(k, sites):
        copies = send_faces(k)
        totals = []
        for group in range(4):
            terms = [[(m, sites[n]) for m, n in local_terms(group * 4 + j)] for j in range(4)]
            totals.append(term_product(group, terms))
        for slots, which in (((4, 0, 1), (0, 2)), ((2, 3), (1,))):
            for slot in slots:
                copies[slot].wait_recv()
                block = faces[k, slot].astype(F32)
                expand([block[:, r * LANES : (r + 1) * LANES] for r in range(RHS)], slot)
            for group in range(4):
                terms = []
                for j in range(4):
                    remote = remote_terms(group * 4 + j)
                    terms.append([(remote[w][0], site_rows(remote[w][1], remote[w][2])) for w in which])
                totals[group] = totals[group] + term_product(group, terms)
        result = []
        for group in range(4):
            total = totals[group]
            for j in range(4):
                block = total[8 * j : 8 * j + 8, LANES * (j // 2) : LANES * (j // 2) + LANES]
                swapped = pltpu.roll(block, RHS, 0)
                signed = jnp.where(upper, -swapped, swapped)
                if j % 2 == 0:
                    new = jnp.where(low, block, pltpu.roll(signed, half, 1))
                else:
                    new = jnp.where(low, pltpu.roll(block, half, 1), signed)
                new = new.astype(BF16).astype(F32)
                s = group * 4 + j
                kept = jnp.where(low, new, -new)
                packed[pl.ds(s, RHS, stride=SITES), :] = kept[:RHS]
                result.append(new)
        for r in range(RHS):
            blocks[k + 1, :, r * LANES : (r + 1) * LANES] = packed[r * SITES : (r + 1) * SITES, :].astype(BF16)
        return result

    mine = pl.ds(pl.multiple_of(me * SITES, SITES), SITES)
    values = []
    loads[4].wait()
    await_bytes(got, rs_recv)
    for r in range(RHS):
        lanes = slice(r * LANES, (r + 1) * LANES)
        total = part[mine, lanes].astype(F32)
        for i in range(len(order)):
            total = total + got[i, :, lanes].astype(F32)
        rounded = total.astype(BF16)
        blocks[0, :, lanes] = rounded
        values.append(rounded.astype(F32))
    expand(values, 5)
    sites = [site_rows(5, s) for s in range(SITES)]
    sites = apply_operator(0, sites)
    apply_operator(1, sites)

    for dz, dy in order:
        pltpu.make_async_remote_copy(
            src_ref=blocks.at[2],
            dst_ref=whole.at[mine],
            send_sem=ag_send,
            recv_sem=ag_recv,
            device_id={"gx": member(dz, dy)},
            device_id_type=pl.DeviceIdType.MESH,
        ).start()
    pltpu.make_async_copy(blocks.at[2], whole.at[mine], ag_recv).start()

    depth = 2 * NV * RHS
    row = lax.broadcasted_iota(jnp.int32, (2 * RHS, depth), 0)
    column = lax.broadcasted_iota(jnp.int32, (2 * RHS, depth), 1)
    wanted = (column >> 6) + ((column >> 5) & 1) * RHS
    signs = jnp.where(row == wanted, 1.0, 0.0).astype(BF16)

    await_bytes(whole, ag_recv)
    picked[...] = lax.dot_general(whole[...], hot[...], TN, preferred_element_type=F32).astype(BF16)
    wide = 2 * LANES
    steps = fine // wide

    def prolong(step, carry):
        chi = lax.div(step, steps)
        lanes = pl.ds(pl.multiple_of(lax.rem(step, steps) * wide, wide), wide)
        base = pl.multiple_of(chi * NV, NV)
        pr = [picked[pl.ds(r * LANES + base, NV), lanes] for r in range(RHS)]
        pi = [picked[pl.ds(r * LANES + 2 * NV + base, NV), lanes] for r in range(RHS)]
        for a in range(SC):
            vr = vec[0, chi, a, :, lanes]
            vi = vec[1, chi, a, :, lanes]
            products = []
            for r in range(RHS):
                products += [vr * pr[r] - vi * pi[r], vr * pi[r] + vi * pr[r]]
            both = jnp.dot(signs, jnp.concatenate(products, axis=0), preferred_element_type=F32)
            out[0, chi, a, :, lanes] = both[:RHS].astype(BF16)
            out[1, chi, a, :, lanes] = both[RHS:].astype(BF16)
        return carry

    lax.fori_loop(0, 2 * steps, prolong, 0, unroll=4)
    await_bytes(got, rs_send)
    await_bytes(whole.at[pl.ds(0, groups - SITES)], ag_send)
    for k in range(2):
        await_bytes(faces.at[k], face_send.at[k])


def per_device(fine_field, null_vectors, aggregate, coarse_links):
    nx = lax.axis_size("gx")
    nz = lax.axis_size("gz")
    fine = fine_field.shape[-1]
    groups = SITES * nx
    peers = nx - 1
    width = RHS * LANES
    dma = pltpu.SemaphoreType.DMA
    return pl.pallas_call(
        functools.partial(kernel, nx, nz),
        out_shape=jax.ShapeDtypeStruct(fine_field.shape, BF16),
        in_specs=[pl.BlockSpec(memory_space=pltpu.HBM)] * 4,
        out_specs=pl.BlockSpec(memory_space=pltpu.VMEM),
        scratch_shapes=[
            pltpu.VMEM((1, fine), jnp.int32),
            pltpu.VMEM(fine_field.shape, BF16),
            pltpu.VMEM((6 * SC, RHS, fine), F32),
            pltpu.VMEM(null_vectors.shape, BF16),
            pltpu.VMEM(coarse_links.shape, BF16),
            pltpu.VMEM((groups, fine), BF16),
            pltpu.VMEM((width, fine), BF16),
            pltpu.VMEM((groups, width), BF16),
            pltpu.VMEM((peers, SITES, width), BF16),
            pltpu.VMEM((6, 2 * RHS * SITES, LANES), F32),
            pltpu.VMEM((2, 5, SITES, RHS * LANES), BF16),
            pltpu.VMEM((3, SITES, RHS * LANES), BF16),
            pltpu.VMEM((RHS * SITES, LANES), F32),
            pltpu.VMEM((groups, RHS * LANES), BF16),
            pltpu.VMEM((RHS * LANES, fine), BF16),
            dma((5,)),
            dma,
            dma,
            dma((2,)),
            dma((2, 5)),
            dma,
            dma,
        ],
        compiler_params=pltpu.CompilerParams(
            collective_id=0, has_side_effects=True, vmem_limit_bytes=48 * 1024 * 1024
        ),
        name="coarse_cycle",
    )(*[pltpu.with_memory_space_constraint(v, pltpu.HBM) for v in (aggregate.reshape(1, fine), fine_field, null_vectors, coarse_links)])


def solution(mesh):
    in_specs = (
        P(None, None, None, None, ("gx", "gz", "ta")),
        P(None, None, None, None, ("gx", "gz", "ta")),
        P(("gx", "gz", "ta")),
        P("gx", None, "gz", "ta", None, None, None),
    )
    out_specs = P(None, None, None, None, ("gx", "gz", "ta"))
    return jax.shard_map(per_device, mesh=mesh, in_specs=in_specs, out_specs=out_specs, check_vma=False)
```

```python
import functools

import jax
import jax.numpy as jnp
from jax import lax
from jax.experimental import pallas as pl
from jax.experimental.pallas import tpu as pltpu
from jax.sharding import PartitionSpec as P

RHS = 4
NV = 32
SC = 6
SITES = 16
LANES = 128
BACK = (1, 0, 3, 2, 4)
FAR_FIRST = (2, 3, 0, 1, 4)
F32 = jnp.float32
BF16 = jnp.bfloat16
NT = (((1,), (1,)), ((), ()))
TN = (((0,), (0,)), ((), ()))


def ring_order(count):
    long = count // 2
    pairs = [(dz, dy) for dz in range(long) for dy in range(2) if (dz, dy) != (0, 0)]
    return sorted(pairs, key=lambda p: -(2 * min(p[0], long - p[0]) + p[1]))


def site_bits(s):
    return (s >> 3) & 1, (s >> 2) & 1, (s >> 1) & 1, s & 1


def site_of(x, y, z, t):
    return ((x * 2 + y) * 2 + z) * 2 + t


def local_terms(s):
    x, y, z, t = site_bits(s)
    return (
        (0, s),
        (1, site_of(x, 1 - y, z, t)),
        (2, site_of(x, 1 - y, z, t)),
        (3 if x == 0 else 4, site_of(1 - x, y, z, t)),
        (5 if z == 0 else 6, site_of(x, y, 1 - z, t)),
        (7 if t == 0 else 8, site_of(x, y, z, 1 - t)),
    )


def remote_terms(s):
    x, y, z, t = site_bits(s)
    return (
        (3, 0, site_of(0, y, z, t)) if x == 1 else (4, 1, site_of(1, y, z, t)),
        (5, 2, site_of(x, y, 0, t)) if z == 1 else (6, 3, site_of(x, y, 1, t)),
        (7, 4, site_of(x, y, z, 0)) if t == 1 else (8, 4, site_of(x, y, z, 1)),
    )


def kernel(
    nx,
    nz,
    agg_hbm,
    field_hbm,
    vec_hbm,
    links_hbm,
    whole,
    vec,
    hot,
    agg,
    field,
    field32,
    links,
    rows,
    part,
    got,
    spread,
    faces,
    blocks,
    packed,
    in_sem,
    rs_send,
    rs_recv,
    face_send,
    face_recv,
    ag_send,
    ag_recv,
):
    def await_bytes(ref, sem):
        pltpu.make_async_copy(ref, ref, sem).wait()

    fine = agg.shape[1]
    tiles = fine // LANES
    me = lax.axis_index("gx")
    my_z = lax.axis_index("gz")
    my_t = lax.axis_index("ta")
    order = ring_order(nx)
    long = nx // 2

    loads = [
        pltpu.make_async_copy(agg_hbm, agg, in_sem.at[0]),
        pltpu.make_async_copy(field_hbm, field, in_sem.at[1]),
        pltpu.make_async_copy(vec_hbm.at[:, 0], vec.at[:, 0], in_sem.at[2]),
        pltpu.make_async_copy(vec_hbm.at[:, 1], vec.at[:, 1], in_sem.at[3]),
        pltpu.make_async_copy(links_hbm, links, in_sem.at[4]),
    ]
    for load in loads[:4]:
        load.start()

    def member(dz, dy):
        z = lax.rem(lax.div(me, 2) + dz, long)
        y = lax.rem(lax.rem(me, 2) + dy, 2)
        return z * 2 + y

    barrier = pltpu.get_barrier_semaphore()
    neighbours = [
        {"gx": lax.rem(me + 1, nx)},
        {"gx": lax.rem(me + nx - 1, nx)},
        {"gz": lax.rem(my_z + 1, nz)},
        {"gz": lax.rem(my_z + nz - 1, nz)},
        {"ta": 1 - my_t},
    ]
    greeted = [{"gx": member(dz, dy)} for dz, dy in order] + neighbours[2:]
    for device in greeted:
        pl.semaphore_signal(barrier, inc=1, device_id=device, device_id_type=pl.DeviceIdType.MESH)

    loads[0].wait()
    groups = hot.shape[0]

    def hot_tile(i, carry):
        lanes = pl.ds(pl.multiple_of(i * LANES, LANES), LANES)
        site = lax.broadcasted_iota(jnp.int32, (groups, LANES), 0)
        hot[:, lanes] = jnp.where(site == agg[:, lanes], 1.0, 0.0).astype(BF16)
        return carry

    lax.fori_loop(0, tiles, hot_tile, 0)

    loads[1].wait()
    for chi in range(2):
        for a in range(SC):
            plane = chi * SC + a
            fr = field[0, chi, a].astype(F32)
            fi = field[1, chi, a].astype(F32)
            field32[plane] = fr
            field32[2 * SC + plane] = fi
            field32[4 * SC + plane] = fr + fi
    loads[2].wait()
    loads[3].wait()

    loads[4].start()

    def project(step, carry):
        chi = lax.div(step, tiles)
        lanes = pl.ds(pl.multiple_of(lax.rem(step, tiles) * LANES, LANES), LANES)
        height = NV // 2
        for part_of in range(2):
            zero = jnp.zeros((height, LANES), F32)
            both, less, more = [zero] * RHS, [zero] * RHS, [zero] * RHS
            for a in range(SC):
                plane = chi * SC + a
                vr = vec[0, chi, a, part_of * height : (part_of + 1) * height, lanes].astype(F32)
                vi = vec[1, chi, a, part_of * height : (part_of + 1) * height, lanes].astype(F32)
                diff, total = vr - vi, vr + vi
                for r in range(RHS):
                    fr = field32[plane, r : r + 1, lanes]
                    fi = field32[2 * SC + plane, r : r + 1, lanes]
                    fs = field32[4 * SC + plane, r : r + 1, lanes]
                    both[r] = both[r] + vr * fs
                    less[r] = less[r] + diff * fi
                    more[r] = more[r] + total * fr
            base = pl.multiple_of(chi * NV + part_of * height, height)
            for r in range(RHS):
                rows[pl.ds(r * LANES + base, height), lanes] = (both[r] - less[r]).astype(BF16)
                rows[pl.ds(r * LANES + 2 * NV + base, height), lanes] = (both[r] - more[r]).astype(BF16)
        return carry

    lax.fori_loop(0, 2 * tiles, project, 0)
    part[...] = lax.dot_general(hot[...], rows[...], NT, preferred_element_type=F32).astype(BF16)
    pl.semaphore_wait(barrier, len(greeted))
    for i, (dz, dy) in enumerate(order):
        peer = member(dz, dy)
        pltpu.make_async_remote_copy(
            src_ref=part.at[pl.ds(pl.multiple_of(peer * SITES, SITES), SITES)],
            dst_ref=got.at[i],
            send_sem=rs_send,
            recv_sem=rs_recv,
            device_id={"gx": peer},
            device_id_type=pl.DeviceIdType.MESH,
        ).start()

    lane = lax.broadcasted_iota(jnp.int32, (8, LANES), 1)
    low = lane < LANES // 2
    low16 = lax.broadcasted_iota(jnp.int32, (SITES, LANES), 1) < LANES // 2
    upper = lax.broadcasted_iota(jnp.int32, (8, LANES), 0) < RHS
    half = LANES // 2

    def expand(values, slot):
        for r in range(RHS):
            v = values[r]
            spread[slot, r * SITES : (r + 1) * SITES, :] = jnp.where(low16, v, -v)
            spread[slot, (RHS + r) * SITES : (RHS + r + 1) * SITES, :] = pltpu.roll(v, half, 1)

    def site_rows(slot, s):
        return spread[slot, pl.ds(s, 2 * RHS, stride=SITES), :]

    def send_faces(k):
        copies = {}
        for i in FAR_FIRST:
            back = BACK[i]
            copy = pltpu.make_async_remote_copy(
                src_ref=blocks.at[k],
                dst_ref=faces.at[k, back],
                send_sem=face_send.at[k],
                recv_sem=face_recv.at[k, back],
                device_id=neighbours[i],
                device_id_type=pl.DeviceIdType.MESH,
            )
            copy.start()
            copies[back] = copy
        return copies

    def term_product(group, terms):
        total = None
        count = len(terms[0])
        for first in range(0, count, 2):
            pick = range(first, min(first + 2, count))
            left = [jnp.concatenate([terms[j][m][1] for j in range(4)], axis=0).astype(BF16) for m in pick]
            right = []
            for m in pick:
                part_links = []
                for j in range(4):
                    x, y, z, t = site_bits(group * 4 + j)
                    part_links.append(links[x, y, z, t, terms[j][m][0]])
                right.append(jnp.concatenate(part_links, axis=0))
            lhs = left[0] if len(left) == 1 else jnp.concatenate(left, axis=1)
            rhs = right[0] if len(right) == 1 else jnp.concatenate(right, axis=1)
            product = lax.dot_general(lhs, rhs, NT, preferred_element_type=F32)
            total = product if total is None else total + product
        return total

    def apply_operator(k, sites):
        copies = send_faces(k)
        totals = []
        for group in range(4):
            terms = [[(m, sites[n]) for m, n in local_terms(group * 4 + j)] for j in range(4)]
            totals.append(term_product(group, terms))
        for slots, which in (((4, 0, 1), (0, 2)), ((2, 3), (1,))):
            for slot in slots:
                copies[slot].wait_recv()
                block = faces[k, slot].astype(F32)
                expand([block[:, r * LANES : (r + 1) * LANES] for r in range(RHS)], slot)
            for group in range(4):
                terms = []
                for j in range(4):
                    remote = remote_terms(group * 4 + j)
                    terms.append([(remote[w][0], site_rows(remote[w][1], remote[w][2])) for w in which])
                totals[group] = totals[group] + term_product(group, terms)
        result = []
        for group in range(4):
            total = totals[group]
            for j in range(4):
                block = total[8 * j : 8 * j + 8, LANES * (j // 2) : LANES * (j // 2) + LANES]
                swapped = pltpu.roll(block, RHS, 0)
                signed = jnp.where(upper, -swapped, swapped)
                if j % 2 == 0:
                    new = jnp.where(low, block, pltpu.roll(signed, half, 1))
                else:
                    new = jnp.where(low, pltpu.roll(block, half, 1), signed)
                new = new.astype(BF16).astype(F32)
                s = group * 4 + j
                kept = jnp.where(low, new, -new)
                packed[pl.ds(s, RHS, stride=SITES), :] = kept[:RHS]
                result.append(new)
        for r in range(RHS):
            blocks[k + 1, :, r * LANES : (r + 1) * LANES] = packed[r * SITES : (r + 1) * SITES, :].astype(BF16)
        return result

    mine = pl.ds(pl.multiple_of(me * SITES, SITES), SITES)
    values = []
    loads[4].wait()
    await_bytes(got, rs_recv)
    for r in range(RHS):
        lanes = slice(r * LANES, (r + 1) * LANES)
        total = part[mine, lanes].astype(F32)
        for i in range(len(order)):
            total = total + got[i, :, lanes].astype(F32)
        rounded = total.astype(BF16)
        blocks[0, :, lanes] = rounded
        values.append(rounded.astype(F32))
    expand(values, 5)
    sites = [site_rows(5, s) for s in range(SITES)]
    sites = apply_operator(0, sites)
    apply_operator(1, sites)

    for dz, dy in order:
        pltpu.make_async_remote_copy(
            src_ref=blocks.at[2],
            dst_ref=whole.at[mine],
            send_sem=ag_send,
            recv_sem=ag_recv,
            device_id={"gx": member(dz, dy)},
            device_id_type=pl.DeviceIdType.MESH,
        ).start()
    pltpu.make_async_copy(blocks.at[2], whole.at[mine], ag_recv).start()

    await_bytes(whole, ag_recv)
    await_bytes(got, rs_send)
    await_bytes(whole.at[pl.ds(0, groups - SITES)], ag_send)
    for k in range(2):
        await_bytes(faces.at[k], face_send.at[k])


def prolong_kernel(whole, vec, hot, out_hbm, picked, out, sem):
    fine = hot.shape[1]
    depth = 2 * NV * RHS
    row = lax.broadcasted_iota(jnp.int32, (2 * RHS, depth), 0)
    column = lax.broadcasted_iota(jnp.int32, (2 * RHS, depth), 1)
    wanted = (column >> 6) + ((column >> 5) & 1) * RHS
    signs = jnp.where(row == wanted, 1.0, 0.0).astype(BF16)

    picked[...] = lax.dot_general(whole[...], hot[...], TN, preferred_element_type=F32).astype(BF16)
    wide = 2 * LANES
    steps = fine // wide

    def prolong(step, carry):
        chi = lax.div(step, steps)
        lanes = pl.ds(pl.multiple_of(lax.rem(step, steps) * wide, wide), wide)
        base = pl.multiple_of(chi * NV, NV)
        pr = [picked[pl.ds(r * LANES + base, NV), lanes] for r in range(RHS)]
        pi = [picked[pl.ds(r * LANES + 2 * NV + base, NV), lanes] for r in range(RHS)]
        for a in range(SC):
            vr = vec[0, chi, a, :, lanes]
            vi = vec[1, chi, a, :, lanes]
            products = []
            for r in range(RHS):
                products += [vr * pr[r] - vi * pi[r], vr * pi[r] + vi * pr[r]]
            both = jnp.dot(signs, jnp.concatenate(products, axis=0), preferred_element_type=F32)
            out[0, chi, a, :, lanes] = both[:RHS].astype(BF16)
            out[1, chi, a, :, lanes] = both[RHS:].astype(BF16)
        return carry

    stores = []
    for i in range(steps):
        for chi in range(2):
            prolong(chi * steps + i, 0)
        lanes = pl.ds(i * wide, wide)
        store = pltpu.make_async_copy(
            out.at[:, :, :, :, lanes], out_hbm.at[:, :, :, :, lanes], sem.at[i]
        )
        store.start()
        stores.append(store)
    for store in stores:
        store.wait()


def per_device(fine_field, null_vectors, aggregate, coarse_links):
    nx = lax.axis_size("gx")
    nz = lax.axis_size("gz")
    fine = fine_field.shape[-1]
    groups = SITES * nx
    peers = nx - 1
    width = RHS * LANES
    dma = pltpu.SemaphoreType.DMA
    vmem = pl.BlockSpec(memory_space=pltpu.VMEM)
    whole, vec, hot = pl.pallas_call(
        functools.partial(kernel, nx, nz),
        out_shape=(
            jax.ShapeDtypeStruct((groups, width), BF16),
            jax.ShapeDtypeStruct(null_vectors.shape, BF16),
            jax.ShapeDtypeStruct((groups, fine), BF16),
        ),
        in_specs=[pl.BlockSpec(memory_space=pltpu.HBM)] * 4,
        out_specs=(vmem, vmem, vmem),
        scratch_shapes=[
            pltpu.VMEM((1, fine), jnp.int32),
            pltpu.VMEM(fine_field.shape, BF16),
            pltpu.VMEM((6 * SC, RHS, fine), F32),
            pltpu.VMEM(coarse_links.shape, BF16),
            pltpu.VMEM((width, fine), BF16),
            pltpu.VMEM((groups, width), BF16),
            pltpu.VMEM((peers, SITES, width), BF16),
            pltpu.VMEM((6, 2 * RHS * SITES, LANES), F32),
            pltpu.VMEM((2, 5, SITES, RHS * LANES), BF16),
            pltpu.VMEM((3, SITES, RHS * LANES), BF16),
            pltpu.VMEM((RHS * SITES, LANES), F32),
            dma((5,)),
            dma,
            dma,
            dma((2,)),
            dma((2, 5)),
            dma,
            dma,
        ],
        compiler_params=pltpu.CompilerParams(
            collective_id=0, has_side_effects=True, vmem_limit_bytes=48 * 1024 * 1024
        ),
        name="coarse_cycle",
    )(*[pltpu.with_memory_space_constraint(v, pltpu.HBM) for v in (aggregate.reshape(1, fine), fine_field, null_vectors, coarse_links)])
    return pl.pallas_call(
        prolong_kernel,
        out_shape=jax.ShapeDtypeStruct(fine_field.shape, BF16),
        in_specs=[vmem] * 3,
        out_specs=pl.BlockSpec(memory_space=pltpu.HBM),
        scratch_shapes=[
            pltpu.VMEM((RHS * LANES, fine), BF16),
            pltpu.VMEM(fine_field.shape, BF16),
            dma((fine // (2 * LANES),)),
        ],
        compiler_params=pltpu.CompilerParams(vmem_limit_bytes=48 * 1024 * 1024),
        name="prolong",
    )(whole, vec, hot)


def solution(mesh):
    in_specs = (
        P(None, None, None, None, ("gx", "gz", "ta")),
        P(None, None, None, None, ("gx", "gz", "ta")),
        P(("gx", "gz", "ta")),
        P("gx", None, "gz", "ta", None, None, None),
    )
    out_specs = P(None, None, None, None, ("gx", "gz", "ta"))
    return jax.shard_map(per_device, mesh=mesh, in_specs=in_specs, out_specs=out_specs, check_vma=False)
```

```python
import functools

import jax
import jax.numpy as jnp
from jax import lax
from jax.experimental import pallas as pl
from jax.experimental.pallas import tpu as pltpu
from jax.sharding import PartitionSpec as P

RHS = 4
NV = 32
SC = 6
SITES = 16
LANES = 128
BACK = (1, 0, 3, 2, 4)
FAR_FIRST = (2, 3, 0, 1, 4)
F32 = jnp.float32
BF16 = jnp.bfloat16
NT = (((1,), (1,)), ((), ()))
TN = (((0,), (0,)), ((), ()))


def ring_order(count):
    long = count // 2
    pairs = [(dz, dy) for dz in range(long) for dy in range(2) if (dz, dy) != (0, 0)]
    return sorted(pairs, key=lambda p: -(2 * min(p[0], long - p[0]) + p[1]))


def site_bits(s):
    return (s >> 3) & 1, (s >> 2) & 1, (s >> 1) & 1, s & 1


def site_of(x, y, z, t):
    return ((x * 2 + y) * 2 + z) * 2 + t


def local_terms(s):
    x, y, z, t = site_bits(s)
    return (
        (0, s),
        (1, site_of(x, 1 - y, z, t)),
        (2, site_of(x, 1 - y, z, t)),
        (3 if x == 0 else 4, site_of(1 - x, y, z, t)),
        (5 if z == 0 else 6, site_of(x, y, 1 - z, t)),
        (7 if t == 0 else 8, site_of(x, y, z, 1 - t)),
    )


def remote_terms(s):
    x, y, z, t = site_bits(s)
    return (
        (3, 0, site_of(0, y, z, t)) if x == 1 else (4, 1, site_of(1, y, z, t)),
        (5, 2, site_of(x, y, 0, t)) if z == 1 else (6, 3, site_of(x, y, 1, t)),
        (7, 4, site_of(x, y, z, 0)) if t == 1 else (8, 4, site_of(x, y, z, 1)),
    )


def kernel(
    nx,
    nz,
    agg_hbm,
    field_hbm,
    vec_hbm,
    links_hbm,
    whole,
    vec,
    hot,
    agg,
    field,
    field32,
    links,
    rows,
    part,
    got,
    spread,
    faces,
    blocks,
    packed,
    in_sem,
    rs_send,
    rs_recv,
    face_send,
    face_recv,
    ag_send,
    ag_recv,
):
    def await_bytes(ref, sem):
        pltpu.make_async_copy(ref, ref, sem).wait()

    fine = agg.shape[1]
    tiles = fine // LANES
    me = lax.axis_index("gx")
    my_z = lax.axis_index("gz")
    my_t = lax.axis_index("ta")
    order = ring_order(nx)
    long = nx // 2

    loads = [
        pltpu.make_async_copy(agg_hbm, agg, in_sem.at[0]),
        pltpu.make_async_copy(field_hbm, field, in_sem.at[1]),
        pltpu.make_async_copy(vec_hbm.at[:, 0], vec.at[:, 0], in_sem.at[2]),
        pltpu.make_async_copy(vec_hbm.at[:, 1], vec.at[:, 1], in_sem.at[3]),
        pltpu.make_async_copy(links_hbm, links, in_sem.at[4]),
    ]
    for load in loads[:4]:
        load.start()

    my_row = lax.div(me, 2)
    my_side = me - 2 * my_row

    def member(dz, dy):
        z = my_row + dz
        z = jnp.where(z >= long, z - long, z)
        y = 1 - my_side if dy == 1 else my_side
        return z * 2 + y

    barrier = pltpu.get_barrier_semaphore()
    neighbours = [
        {"gx": lax.rem(me + 1, nx)},
        {"gx": lax.rem(me + nx - 1, nx)},
        {"gz": lax.rem(my_z + 1, nz)},
        {"gz": lax.rem(my_z + nz - 1, nz)},
        {"ta": 1 - my_t},
    ]
    greeted = [{"gx": member(dz, dy)} for dz, dy in order] + neighbours[2:]
    for device in greeted:
        pl.semaphore_signal(barrier, inc=1, device_id=device, device_id_type=pl.DeviceIdType.MESH)

    loads[0].wait()
    groups = hot.shape[0]

    def hot_tile(i, carry):
        lanes = pl.ds(pl.multiple_of(i * LANES, LANES), LANES)
        site = lax.broadcasted_iota(jnp.int32, (groups, LANES), 0)
        hot[:, lanes] = jnp.where(site == agg[:, lanes], 1.0, 0.0).astype(BF16)
        return carry

    lax.fori_loop(0, tiles, hot_tile, 0)

    loads[1].wait()
    for chi in range(2):
        for a in range(SC):
            plane = chi * SC + a
            fr = field[0, chi, a].astype(F32)
            fi = field[1, chi, a].astype(F32)
            field32[plane] = fr
            field32[2 * SC + plane] = fi
            field32[4 * SC + plane] = fr + fi
    loads[2].wait()
    loads[3].wait()

    loads[4].start()

    def project(step, carry):
        chi = lax.div(step, tiles)
        lanes = pl.ds(pl.multiple_of(lax.rem(step, tiles) * LANES, LANES), LANES)
        height = NV // 2
        for part_of in range(2):
            zero = jnp.zeros((height, LANES), F32)
            both, less, more = [zero] * RHS, [zero] * RHS, [zero] * RHS
            for a in range(SC):
                plane = chi * SC + a
                vr = vec[0, chi, a, part_of * height : (part_of + 1) * height, lanes].astype(F32)
                vi = vec[1, chi, a, part_of * height : (part_of + 1) * height, lanes].astype(F32)
                diff, total = vr - vi, vr + vi
                for r in range(RHS):
                    fr = field32[plane, r : r + 1, lanes]
                    fi = field32[2 * SC + plane, r : r + 1, lanes]
                    fs = field32[4 * SC + plane, r : r + 1, lanes]
                    both[r] = both[r] + vr * fs
                    less[r] = less[r] + diff * fi
                    more[r] = more[r] + total * fr
            base = pl.multiple_of(chi * NV + part_of * height, height)
            for r in range(RHS):
                rows[pl.ds(r * LANES + base, height), lanes] = (both[r] - less[r]).astype(BF16)
                rows[pl.ds(r * LANES + 2 * NV + base, height), lanes] = (both[r] - more[r]).astype(BF16)
        return carry

    lax.fori_loop(0, 2 * tiles, project, 0)
    part[...] = lax.dot_general(hot[...], rows[...], NT, preferred_element_type=F32).astype(BF16)
    pl.semaphore_wait(barrier, len(greeted))
    for i, (dz, dy) in enumerate(order):
        peer = member(dz, dy)
        pltpu.make_async_remote_copy(
            src_ref=part.at[pl.ds(pl.multiple_of(peer * SITES, SITES), SITES)],
            dst_ref=got.at[i],
            send_sem=rs_send,
            recv_sem=rs_recv,
            device_id={"gx": peer},
            device_id_type=pl.DeviceIdType.MESH,
        ).start()

    lane = lax.broadcasted_iota(jnp.int32, (8, LANES), 1)
    low = lane < LANES // 2
    low16 = lax.broadcasted_iota(jnp.int32, (SITES, LANES), 1) < LANES // 2
    upper = lax.broadcasted_iota(jnp.int32, (8, LANES), 0) < RHS
    half = LANES // 2

    def expand(values, slot):
        for r in range(RHS):
            v = values[r]
            spread[slot, r * SITES : (r + 1) * SITES, :] = jnp.where(low16, v, -v)
            spread[slot, (RHS + r) * SITES : (RHS + r + 1) * SITES, :] = pltpu.roll(v, half, 1)

    def site_rows(slot, s):
        return spread[slot, pl.ds(s, 2 * RHS, stride=SITES), :]

    def send_faces(k):
        copies = {}
        for i in FAR_FIRST:
            back = BACK[i]
            copy = pltpu.make_async_remote_copy(
                src_ref=blocks.at[k],
                dst_ref=faces.at[k, back],
                send_sem=face_send.at[k],
                recv_sem=face_recv.at[k, back],
                device_id=neighbours[i],
                device_id_type=pl.DeviceIdType.MESH,
            )
            copy.start()
            copies[back] = copy
        return copies

    def term_product(group, terms):
        total = None
        count = len(terms[0])
        for first in range(0, count, 2):
            pick = range(first, min(first + 2, count))
            left = [jnp.concatenate([terms[j][m][1] for j in range(4)], axis=0).astype(BF16) for m in pick]
            right = []
            for m in pick:
                part_links = []
                for j in range(4):
                    x, y, z, t = site_bits(group * 4 + j)
                    part_links.append(links[x, y, z, t, terms[j][m][0]])
                right.append(jnp.concatenate(part_links, axis=0))
            lhs = left[0] if len(left) == 1 else jnp.concatenate(left, axis=1)
            rhs = right[0] if len(right) == 1 else jnp.concatenate(right, axis=1)
            product = lax.dot_general(lhs, rhs, NT, preferred_element_type=F32)
            total = product if total is None else total + product
        return total

    def apply_operator(k, sites):
        copies = send_faces(k)
        totals = []
        for group in range(4):
            terms = [[(m, sites[n]) for m, n in local_terms(group * 4 + j)] for j in range(4)]
            totals.append(term_product(group, terms))
        for slots, which in (((4, 0, 1), (0, 2)), ((2, 3), (1,))):
            for slot in slots:
                copies[slot].wait_recv()
                block = faces[k, slot].astype(F32)
                expand([block[:, r * LANES : (r + 1) * LANES] for r in range(RHS)], slot)
            for group in range(4):
                terms = []
                for j in range(4):
                    remote = remote_terms(group * 4 + j)
                    terms.append([(remote[w][0], site_rows(remote[w][1], remote[w][2])) for w in which])
                totals[group] = totals[group] + term_product(group, terms)
        result = []
        for group in range(4):
            total = totals[group]
            for j in range(4):
                block = total[8 * j : 8 * j + 8, LANES * (j // 2) : LANES * (j // 2) + LANES]
                swapped = pltpu.roll(block, RHS, 0)
                signed = jnp.where(upper, -swapped, swapped)
                if j % 2 == 0:
                    new = jnp.where(low, block, pltpu.roll(signed, half, 1))
                else:
                    new = jnp.where(low, pltpu.roll(block, half, 1), signed)
                new = new.astype(BF16).astype(F32)
                s = group * 4 + j
                kept = jnp.where(low, new, -new)
                packed[pl.ds(s, RHS, stride=SITES), :] = kept[:RHS]
                result.append(new)
        for r in range(RHS):
            blocks[k + 1, :, r * LANES : (r + 1) * LANES] = packed[r * SITES : (r + 1) * SITES, :].astype(BF16)
        return result

    mine = pl.ds(pl.multiple_of(me * SITES, SITES), SITES)
    values = []
    loads[4].wait()
    await_bytes(got, rs_recv)
    for r in range(RHS):
        lanes = slice(r * LANES, (r + 1) * LANES)
        total = part[mine, lanes].astype(F32)
        for i in range(len(order)):
            total = total + got[i, :, lanes].astype(F32)
        rounded = total.astype(BF16)
        blocks[0, :, lanes] = rounded
        values.append(rounded.astype(F32))
    expand(values, 5)
    sites = [site_rows(5, s) for s in range(SITES)]
    sites = apply_operator(0, sites)
    apply_operator(1, sites)

    for dz, dy in order:
        pltpu.make_async_remote_copy(
            src_ref=blocks.at[2],
            dst_ref=whole.at[mine],
            send_sem=ag_send,
            recv_sem=ag_recv,
            device_id={"gx": member(dz, dy)},
            device_id_type=pl.DeviceIdType.MESH,
        ).start()
    pltpu.make_async_copy(blocks.at[2], whole.at[mine], ag_recv).start()

    await_bytes(whole, ag_recv)
    await_bytes(got, rs_send)
    await_bytes(whole.at[pl.ds(0, groups - SITES)], ag_send)
    for k in range(2):
        await_bytes(faces.at[k], face_send.at[k])


def prolong_kernel(whole, vec, hot, out_hbm, picked, out, sem):
    fine = hot.shape[1]
    depth = 2 * NV * RHS
    row = lax.broadcasted_iota(jnp.int32, (2 * RHS, depth), 0)
    column = lax.broadcasted_iota(jnp.int32, (2 * RHS, depth), 1)
    wanted = (column >> 6) + ((column >> 5) & 1) * RHS
    signs = jnp.where(row == wanted, 1.0, 0.0).astype(BF16)

    picked[...] = lax.dot_general(whole[...], hot[...], TN, preferred_element_type=F32).astype(BF16)
    wide = 2 * LANES
    steps = fine // wide

    def prolong(step, carry):
        chi = lax.div(step, steps)
        lanes = pl.ds(pl.multiple_of(lax.rem(step, steps) * wide, wide), wide)
        base = pl.multiple_of(chi * NV, NV)
        pr = [picked[pl.ds(r * LANES + base, NV), lanes] for r in range(RHS)]
        pi = [picked[pl.ds(r * LANES + 2 * NV + base, NV), lanes] for r in range(RHS)]
        for a in range(SC):
            vr = vec[0, chi, a, :, lanes]
            vi = vec[1, chi, a, :, lanes]
            products = []
            for r in range(RHS):
                products += [vr * pr[r] - vi * pi[r], vr * pi[r] + vi * pr[r]]
            both = jnp.dot(signs, jnp.concatenate(products, axis=0), preferred_element_type=F32)
            out[0, chi, a, :, lanes] = both[:RHS].astype(BF16)
            out[1, chi, a, :, lanes] = both[RHS:].astype(BF16)
        return carry

    stores = []
    for i in range(steps):
        for chi in range(2):
            prolong(chi * steps + i, 0)
        lanes = pl.ds(i * wide, wide)
        store = pltpu.make_async_copy(
            out.at[:, :, :, :, lanes], out_hbm.at[:, :, :, :, lanes], sem.at[i]
        )
        store.start()
        stores.append(store)
    for store in stores:
        store.wait()


def per_device(fine_field, null_vectors, aggregate, coarse_links):
    nx = lax.axis_size("gx")
    nz = lax.axis_size("gz")
    fine = fine_field.shape[-1]
    groups = SITES * nx
    peers = nx - 1
    width = RHS * LANES
    dma = pltpu.SemaphoreType.DMA
    vmem = pl.BlockSpec(memory_space=pltpu.VMEM)
    whole, vec, hot = pl.pallas_call(
        functools.partial(kernel, nx, nz),
        out_shape=(
            jax.ShapeDtypeStruct((groups, width), BF16),
            jax.ShapeDtypeStruct(null_vectors.shape, BF16),
            jax.ShapeDtypeStruct((groups, fine), BF16),
        ),
        in_specs=[pl.BlockSpec(memory_space=pltpu.HBM)] * 4,
        out_specs=(vmem, vmem, vmem),
        scratch_shapes=[
            pltpu.VMEM((1, fine), jnp.int32),
            pltpu.VMEM(fine_field.shape, BF16),
            pltpu.VMEM((6 * SC, RHS, fine), F32),
            pltpu.VMEM(coarse_links.shape, BF16),
            pltpu.VMEM((width, fine), BF16),
            pltpu.VMEM((groups, width), BF16),
            pltpu.VMEM((peers, SITES, width), BF16),
            pltpu.VMEM((6, 2 * RHS * SITES, LANES), F32),
            pltpu.VMEM((2, 5, SITES, RHS * LANES), BF16),
            pltpu.VMEM((3, SITES, RHS * LANES), BF16),
            pltpu.VMEM((RHS * SITES, LANES), F32),
            dma((5,)),
            dma,
            dma,
            dma((2,)),
            dma((2, 5)),
            dma,
            dma,
        ],
        compiler_params=pltpu.CompilerParams(
            collective_id=0, has_side_effects=True, vmem_limit_bytes=48 * 1024 * 1024
        ),
        name="coarse_cycle",
    )(*[pltpu.with_memory_space_constraint(v, pltpu.HBM) for v in (aggregate.reshape(1, fine), fine_field, null_vectors, coarse_links)])
    return pl.pallas_call(
        prolong_kernel,
        out_shape=jax.ShapeDtypeStruct(fine_field.shape, BF16),
        in_specs=[vmem] * 3,
        out_specs=pl.BlockSpec(memory_space=pltpu.HBM),
        scratch_shapes=[
            pltpu.VMEM((RHS * LANES, fine), BF16),
            pltpu.VMEM(fine_field.shape, BF16),
            dma((fine // (2 * LANES),)),
        ],
        compiler_params=pltpu.CompilerParams(vmem_limit_bytes=48 * 1024 * 1024),
        name="prolong",
    )(whole, vec, hot)


def solution(mesh):
    in_specs = (
        P(None, None, None, None, ("gx", "gz", "ta")),
        P(None, None, None, None, ("gx", "gz", "ta")),
        P(("gx", "gz", "ta")),
        P("gx", None, "gz", "ta", None, None, None),
    )
    out_specs = P(None, None, None, None, ("gx", "gz", "ta"))
    return jax.shard_map(per_device, mesh=mesh, in_specs=in_specs, out_specs=out_specs, check_vma=False)
```

```python
import functools

import jax
import jax.numpy as jnp
from jax import lax
from jax.experimental import pallas as pl
from jax.experimental.pallas import tpu as pltpu
from jax.sharding import PartitionSpec as P

RHS = 4
NV = 32
SC = 6
SITES = 16
LANES = 128
BACK = (1, 0, 3, 2, 4)
FAR_FIRST = (2, 3, 0, 1, 4)
F32 = jnp.float32
BF16 = jnp.bfloat16
NT = (((1,), (1,)), ((), ()))
TN = (((0,), (0,)), ((), ()))


def ring_order(count):
    long = count // 2
    pairs = [(dz, dy) for dz in range(long) for dy in range(2) if (dz, dy) != (0, 0)]
    return sorted(pairs, key=lambda p: -(2 * min(p[0], long - p[0]) + p[1]))


def site_bits(s):
    return (s >> 3) & 1, (s >> 2) & 1, (s >> 1) & 1, s & 1


def site_of(x, y, z, t):
    return ((x * 2 + y) * 2 + z) * 2 + t


def local_terms(s):
    x, y, z, t = site_bits(s)
    return (
        (0, s),
        (1, site_of(x, 1 - y, z, t)),
        (2, site_of(x, 1 - y, z, t)),
        (3 if x == 0 else 4, site_of(1 - x, y, z, t)),
        (5 if z == 0 else 6, site_of(x, y, 1 - z, t)),
        (7 if t == 0 else 8, site_of(x, y, z, 1 - t)),
    )


def remote_terms(s):
    x, y, z, t = site_bits(s)
    return (
        (3, 0, site_of(0, y, z, t)) if x == 1 else (4, 1, site_of(1, y, z, t)),
        (5, 2, site_of(x, y, 0, t)) if z == 1 else (6, 3, site_of(x, y, 1, t)),
        (7, 4, site_of(x, y, z, 0)) if t == 1 else (8, 4, site_of(x, y, z, 1)),
    )


def kernel(
    nx,
    nz,
    agg_hbm,
    field_hbm,
    vec_hbm,
    links_hbm,
    whole,
    vec,
    hot,
    agg,
    field,
    field32,
    links,
    rows,
    part,
    got,
    spread,
    faces,
    blocks,
    packed,
    in_sem,
    rs_send,
    rs_recv,
    face_send,
    face_recv,
    ag_send,
    ag_recv,
):
    def await_bytes(ref, sem):
        pltpu.make_async_copy(ref, ref, sem).wait()

    fine = agg.shape[1]
    tiles = fine // LANES
    me = lax.axis_index("gx")
    my_z = lax.axis_index("gz")
    my_t = lax.axis_index("ta")
    order = ring_order(nx)
    long = nx // 2

    loads = [
        pltpu.make_async_copy(agg_hbm, agg, in_sem.at[0]),
        pltpu.make_async_copy(field_hbm, field, in_sem.at[1]),
        pltpu.make_async_copy(vec_hbm.at[:, 0], vec.at[:, 0], in_sem.at[2]),
        pltpu.make_async_copy(vec_hbm.at[:, 1], vec.at[:, 1], in_sem.at[3]),
        pltpu.make_async_copy(links_hbm, links, in_sem.at[4]),
    ]
    for load in loads[:4]:
        load.start()

    def member(dz, dy):
        z = lax.rem(lax.div(me, 2) + dz, long)
        y = lax.rem(lax.rem(me, 2) + dy, 2)
        return z * 2 + y

    barrier = pltpu.get_barrier_semaphore()
    neighbours = [
        {"gx": lax.rem(me + 1, nx)},
        {"gx": lax.rem(me + nx - 1, nx)},
        {"gz": lax.rem(my_z + 1, nz)},
        {"gz": lax.rem(my_z + nz - 1, nz)},
        {"ta": 1 - my_t},
    ]
    greeted = [{"gx": member(dz, dy)} for dz, dy in order] + neighbours[2:]
    for device in greeted:
        pl.semaphore_signal(barrier, inc=1, device_id=device, device_id_type=pl.DeviceIdType.MESH)

    loads[0].wait()
    groups = hot.shape[0]

    def hot_tile(i, carry):
        lanes = pl.ds(pl.multiple_of(i * LANES, LANES), LANES)
        site = lax.broadcasted_iota(jnp.int32, (groups, LANES), 0)
        hot[:, lanes] = jnp.where(site == agg[:, lanes], 1.0, 0.0).astype(BF16)
        return carry

    lax.fori_loop(0, tiles, hot_tile, 0)

    loads[1].wait()
    for chi in range(2):
        for a in range(SC):
            plane = chi * SC + a
            fr = field[0, chi, a].astype(F32)
            fi = field[1, chi, a].astype(F32)
            field32[plane] = fr
            field32[2 * SC + plane] = fi
            field32[4 * SC + plane] = fr + fi
    loads[2].wait()

    def project(step, carry):
        chi = lax.div(step, tiles)
        lanes = pl.ds(pl.multiple_of(lax.rem(step, tiles) * LANES, LANES), LANES)
        height = NV // 2
        for part_of in range(2):
            zero = jnp.zeros((height, LANES), F32)
            both, less, more = [zero] * RHS, [zero] * RHS, [zero] * RHS
            for a in range(SC):
                plane = chi * SC + a
                vr = vec[0, chi, a, part_of * height : (part_of + 1) * height, lanes].astype(F32)
                vi = vec[1, chi, a, part_of * height : (part_of + 1) * height, lanes].astype(F32)
                diff, total = vr - vi, vr + vi
                for r in range(RHS):
                    fr = field32[plane, r : r + 1, lanes]
                    fi = field32[2 * SC + plane, r : r + 1, lanes]
                    fs = field32[4 * SC + plane, r : r + 1, lanes]
                    both[r] = both[r] + vr * fs
                    less[r] = less[r] + diff * fi
                    more[r] = more[r] + total * fr
            base = pl.multiple_of(chi * NV + part_of * height, height)
            for r in range(RHS):
                rows[pl.ds(r * LANES + base, height), lanes] = (both[r] - less[r]).astype(BF16)
                rows[pl.ds(r * LANES + 2 * NV + base, height), lanes] = (both[r] - more[r]).astype(BF16)
        return carry

    lax.fori_loop(0, tiles, project, 0)
    loads[3].wait()
    loads[4].start()
    lax.fori_loop(tiles, 2 * tiles, project, 0)
    part[...] = lax.dot_general(hot[...], rows[...], NT, preferred_element_type=F32).astype(BF16)
    pl.semaphore_wait(barrier, len(greeted))
    for i, (dz, dy) in enumerate(order):
        peer = member(dz, dy)
        pltpu.make_async_remote_copy(
            src_ref=part.at[pl.ds(pl.multiple_of(peer * SITES, SITES), SITES)],
            dst_ref=got.at[i],
            send_sem=rs_send,
            recv_sem=rs_recv,
            device_id={"gx": peer},
            device_id_type=pl.DeviceIdType.MESH,
        ).start()

    lane = lax.broadcasted_iota(jnp.int32, (8, LANES), 1)
    low = lane < LANES // 2
    low16 = lax.broadcasted_iota(jnp.int32, (SITES, LANES), 1) < LANES // 2
    upper = lax.broadcasted_iota(jnp.int32, (8, LANES), 0) < RHS
    half = LANES // 2

    def expand(values, slot):
        for r in range(RHS):
            v = values[r]
            spread[slot, r * SITES : (r + 1) * SITES, :] = jnp.where(low16, v, -v)
            spread[slot, (RHS + r) * SITES : (RHS + r + 1) * SITES, :] = pltpu.roll(v, half, 1)

    def site_rows(slot, s):
        return spread[slot, pl.ds(s, 2 * RHS, stride=SITES), :]

    def send_faces(k):
        copies = {}
        for i in FAR_FIRST:
            back = BACK[i]
            copy = pltpu.make_async_remote_copy(
                src_ref=blocks.at[k],
                dst_ref=faces.at[k, back],
                send_sem=face_send.at[k],
                recv_sem=face_recv.at[k, back],
                device_id=neighbours[i],
                device_id_type=pl.DeviceIdType.MESH,
            )
            copy.start()
            copies[back] = copy
        return copies

    def term_product(group, terms):
        total = None
        count = len(terms[0])
        for first in range(0, count, 2):
            pick = range(first, min(first + 2, count))
            left = [jnp.concatenate([terms[j][m][1] for j in range(4)], axis=0).astype(BF16) for m in pick]
            right = []
            for m in pick:
                part_links = []
                for j in range(4):
                    x, y, z, t = site_bits(group * 4 + j)
                    part_links.append(links[x, y, z, t, terms[j][m][0]])
                right.append(jnp.concatenate(part_links, axis=0))
            lhs = left[0] if len(left) == 1 else jnp.concatenate(left, axis=1)
            rhs = right[0] if len(right) == 1 else jnp.concatenate(right, axis=1)
            product = lax.dot_general(lhs, rhs, NT, preferred_element_type=F32)
            total = product if total is None else total + product
        return total

    def apply_operator(k, sites):
        copies = send_faces(k)
        totals = []
        for group in range(4):
            terms = [[(m, sites[n]) for m, n in local_terms(group * 4 + j)] for j in range(4)]
            totals.append(term_product(group, terms))
        for slots, which in (((4, 0, 1), (0, 2)), ((2, 3), (1,))):
            for slot in slots:
                copies[slot].wait_recv()
                block = faces[k, slot].astype(F32)
                expand([block[:, r * LANES : (r + 1) * LANES] for r in range(RHS)], slot)
            for group in range(4):
                terms = []
                for j in range(4):
                    remote = remote_terms(group * 4 + j)
                    terms.append([(remote[w][0], site_rows(remote[w][1], remote[w][2])) for w in which])
                totals[group] = totals[group] + term_product(group, terms)
        result = []
        for group in range(4):
            total = totals[group]
            for j in range(4):
                block = total[8 * j : 8 * j + 8, LANES * (j // 2) : LANES * (j // 2) + LANES]
                swapped = pltpu.roll(block, RHS, 0)
                signed = jnp.where(upper, -swapped, swapped)
                if j % 2 == 0:
                    new = jnp.where(low, block, pltpu.roll(signed, half, 1))
                else:
                    new = jnp.where(low, pltpu.roll(block, half, 1), signed)
                new = new.astype(BF16).astype(F32)
                s = group * 4 + j
                kept = jnp.where(low, new, -new)
                packed[pl.ds(s, RHS, stride=SITES), :] = kept[:RHS]
                result.append(new)
        for r in range(RHS):
            blocks[k + 1, :, r * LANES : (r + 1) * LANES] = packed[r * SITES : (r + 1) * SITES, :].astype(BF16)
        return result

    mine = pl.ds(pl.multiple_of(me * SITES, SITES), SITES)
    values = []
    loads[4].wait()
    await_bytes(got, rs_recv)
    for r in range(RHS):
        lanes = slice(r * LANES, (r + 1) * LANES)
        total = part[mine, lanes].astype(F32)
        for i in range(len(order)):
            total = total + got[i, :, lanes].astype(F32)
        rounded = total.astype(BF16)
        blocks[0, :, lanes] = rounded
        values.append(rounded.astype(F32))
    expand(values, 5)
    sites = [site_rows(5, s) for s in range(SITES)]
    sites = apply_operator(0, sites)
    apply_operator(1, sites)

    for dz, dy in order:
        pltpu.make_async_remote_copy(
            src_ref=blocks.at[2],
            dst_ref=whole.at[mine],
            send_sem=ag_send,
            recv_sem=ag_recv,
            device_id={"gx": member(dz, dy)},
            device_id_type=pl.DeviceIdType.MESH,
        ).start()
    pltpu.make_async_copy(blocks.at[2], whole.at[mine], ag_recv).start()

    await_bytes(whole, ag_recv)
    await_bytes(got, rs_send)
    await_bytes(whole.at[pl.ds(0, groups - SITES)], ag_send)
    for k in range(2):
        await_bytes(faces.at[k], face_send.at[k])


def prolong_kernel(whole, vec, hot, out_hbm, picked, out, sem):
    fine = hot.shape[1]
    depth = 2 * NV * RHS
    row = lax.broadcasted_iota(jnp.int32, (2 * RHS, depth), 0)
    column = lax.broadcasted_iota(jnp.int32, (2 * RHS, depth), 1)
    wanted = (column >> 6) + ((column >> 5) & 1) * RHS
    signs = jnp.where(row == wanted, 1.0, 0.0).astype(BF16)

    picked[...] = lax.dot_general(whole[...], hot[...], TN, preferred_element_type=F32).astype(BF16)
    wide = 2 * LANES
    steps = fine // wide

    def prolong(step, carry):
        chi = lax.div(step, steps)
        lanes = pl.ds(pl.multiple_of(lax.rem(step, steps) * wide, wide), wide)
        base = pl.multiple_of(chi * NV, NV)
        pr = [picked[pl.ds(r * LANES + base, NV), lanes] for r in range(RHS)]
        pi = [picked[pl.ds(r * LANES + 2 * NV + base, NV), lanes] for r in range(RHS)]
        for a in range(SC):
            vr = vec[0, chi, a, :, lanes]
            vi = vec[1, chi, a, :, lanes]
            products = []
            for r in range(RHS):
                products += [vr * pr[r] - vi * pi[r], vr * pi[r] + vi * pr[r]]
            both = jnp.dot(signs, jnp.concatenate(products, axis=0), preferred_element_type=F32)
            out[0, chi, a, :, lanes] = both[:RHS].astype(BF16)
            out[1, chi, a, :, lanes] = both[RHS:].astype(BF16)
        return carry

    stores = []
    for i in range(steps):
        for chi in range(2):
            prolong(chi * steps + i, 0)
        lanes = pl.ds(i * wide, wide)
        store = pltpu.make_async_copy(
            out.at[:, :, :, :, lanes], out_hbm.at[:, :, :, :, lanes], sem.at[i]
        )
        store.start()
        stores.append(store)
    for store in stores:
        store.wait()


def per_device(fine_field, null_vectors, aggregate, coarse_links):
    nx = lax.axis_size("gx")
    nz = lax.axis_size("gz")
    fine = fine_field.shape[-1]
    groups = SITES * nx
    peers = nx - 1
    width = RHS * LANES
    dma = pltpu.SemaphoreType.DMA
    vmem = pl.BlockSpec(memory_space=pltpu.VMEM)
    whole, vec, hot = pl.pallas_call(
        functools.partial(kernel, nx, nz),
        out_shape=(
            jax.ShapeDtypeStruct((groups, width), BF16),
            jax.ShapeDtypeStruct(null_vectors.shape, BF16),
            jax.ShapeDtypeStruct((groups, fine), BF16),
        ),
        in_specs=[pl.BlockSpec(memory_space=pltpu.HBM)] * 4,
        out_specs=(vmem, vmem, vmem),
        scratch_shapes=[
            pltpu.VMEM((1, fine), jnp.int32),
            pltpu.VMEM(fine_field.shape, BF16),
            pltpu.VMEM((6 * SC, RHS, fine), F32),
            pltpu.VMEM(coarse_links.shape, BF16),
            pltpu.VMEM((width, fine), BF16),
            pltpu.VMEM((groups, width), BF16),
            pltpu.VMEM((peers, SITES, width), BF16),
            pltpu.VMEM((6, 2 * RHS * SITES, LANES), F32),
            pltpu.VMEM((2, 5, SITES, RHS * LANES), BF16),
            pltpu.VMEM((3, SITES, RHS * LANES), BF16),
            pltpu.VMEM((RHS * SITES, LANES), F32),
            dma((5,)),
            dma,
            dma,
            dma((2,)),
            dma((2, 5)),
            dma,
            dma,
        ],
        compiler_params=pltpu.CompilerParams(
            collective_id=0, has_side_effects=True, vmem_limit_bytes=48 * 1024 * 1024
        ),
        name="coarse_cycle",
    )(*[pltpu.with_memory_space_constraint(v, pltpu.HBM) for v in (aggregate.reshape(1, fine), fine_field, null_vectors, coarse_links)])
    return pl.pallas_call(
        prolong_kernel,
        out_shape=jax.ShapeDtypeStruct(fine_field.shape, BF16),
        in_specs=[vmem] * 3,
        out_specs=pl.BlockSpec(memory_space=pltpu.HBM),
        scratch_shapes=[
            pltpu.VMEM((RHS * LANES, fine), BF16),
            pltpu.VMEM(fine_field.shape, BF16),
            dma((fine // (2 * LANES),)),
        ],
        compiler_params=pltpu.CompilerParams(vmem_limit_bytes=48 * 1024 * 1024),
        name="prolong",
    )(whole, vec, hot)


def solution(mesh):
    in_specs = (
        P(None, None, None, None, ("gx", "gz", "ta")),
        P(None, None, None, None, ("gx", "gz", "ta")),
        P(("gx", "gz", "ta")),
        P("gx", None, "gz", "ta", None, None, None),
    )
    out_specs = P(None, None, None, None, ("gx", "gz", "ta"))
    return jax.shard_map(per_device, mesh=mesh, in_specs=in_specs, out_specs=out_specs, check_vma=False)
```
